512 devices in a mesh: lon: 32 (over z, x), lat: 16 (over y, core).
Axes of the slice: x: 4, y: 8, z: 8, core: 2. Of those that a mesh axis runs over, the one named last changes fastest.
Arguments:
- right_side: float32 [2, 32, 256, 4096], P(None, None, 'lat', 'lon'), may hold values from -36 to 36
- sea_mask: int32 [32, 256, 4096], P(None, 'lat', 'lon'), may hold values 0 or 1
- levels: int32 [256, 4096], P('lat', 'lon'), may hold values from 0 to 32
- east_diffusivity: bfloat16 [32, 256, 4096], P(None, 'lat', 'lon'), may hold values from 1 to 8
- north_diffusivity: bfloat16 [32, 256, 4096], P(None, 'lat', 'lon'), may hold values from 1 to 8
- vertical_diffusivity: bfloat16 [32, 256, 4096], P(None, 'lat', 'lon'), may hold values from 0.5 to 8
Outputs:
- solution_field: float32 [2, 32, 256, 4096], P(None, None, 'lat', 'lon')
- residual: float32 [2, 32, 256, 4096], P(None, None, 'lat', 'lon')
The draws below stay inside these ranges and needn't reach their ends.
All inputs are finite; a program needn't handle non-finite values. No bound on the sum of `sea_mask` on one device may be relied on, other than what follows from the above.
Results may differ from the reference program's by a relative error of at most 0.004.
Values sent between devices are 32-bit elements; how exact they have to be, the bound alone decides.
A program may use at most 64 MiB of HBM per device.

```python
import math
import jax
import jax.numpy as jnp
from jax import lax

NZ = 32
TRACERS = 2
ITERS = 2
NLON = 4096
NLAT = 256


def draw_right_side(key, part):
    lat_pos = jnp.arange(NLAT, dtype=jnp.float32)[:, None] / max(NLAT - 1, 1)
    lon_pos = jnp.arange(NLON, dtype=jnp.float32)[None, :] / max(NLON - 1, 1)
    scales = jnp.exp(math.log(3.0) * (lat_pos + lon_pos))
    shape = (TRACERS, NZ, NLAT, NLON)
    rough = jnp.clip(jax.random.normal(key, shape, jnp.float32), -4.0, 4.0)
    return (rough * scales[None, None]).astype(jnp.float32)


def with_ends(array, key, low, top_value):
    longest = array.shape.index(max(array.shape))
    spots = []
    for shift in (0, 1):
        where = [jax.random.randint(jax.random.fold_in(key, axis), (), 0, length) for axis, length in enumerate(array.shape)]
        where[longest] = (where[longest] + shift) % array.shape[longest]
        spots.append(tuple(where))
    return array.at[spots[0]].set(low).at[spots[1]].set(top_value)


def block_scale(key, shape, split, low, high):
    def one(axis_at, parts):
        steps = jax.random.uniform(jax.random.fold_in(jax.random.fold_in(key, 6), axis_at), (parts,), jnp.float32, low / len(split), high / len(split))
        return jnp.repeat(jnp.exp(steps), shape[axis_at] // parts).reshape((-1,) + (1,) * (len(shape) - axis_at - 1))

    loudness = one(*split[0])
    for cut in split[1:]:
        loudness = loudness * one(*cut)
    return loudness


def setup_inputs(seed: int = 0) -> dict:
    key_list = jax.random.split(jax.random.key(seed), 7)
    return {
        "right_side": draw_right_side(jax.random.fold_in(key_list[6], 71), 0),
        "sea_mask": with_ends((jax.random.randint(key_list[1], (NZ, NLAT, NLON), 0, 10) < 9).astype(jnp.int32), jax.random.fold_in(key_list[1], 1), 0, 1),
        "levels": with_ends(jax.random.randint(key_list[2], (NLAT, NLON), 0, NZ + 1), jax.random.fold_in(key_list[2], 1), 0, NZ).astype(jnp.int32),
        "east_diffusivity": jnp.clip(jnp.exp(math.log(8.0) - 2.0794415 * jax.random.uniform(key_list[3], (NZ, NLAT, NLON), jnp.float32) ** block_scale(key_list[3], (NZ, NLAT, NLON), ((1, 16), (2, 32)), -0.2, 0.2)), 1.0, 8.0).astype(jnp.bfloat16),
        "north_diffusivity": jnp.clip(jnp.exp(math.log(8.0) - 2.0794415 * jax.random.uniform(key_list[4], (NZ, NLAT, NLON), jnp.float32) ** block_scale(key_list[4], (NZ, NLAT, NLON), ((1, 16), (2, 32)), -0.2, 0.2)), 1.0, 8.0).astype(jnp.bfloat16),
        "vertical_diffusivity": jnp.clip(jnp.exp(math.log(8.0) - 2.7725887 * jax.random.uniform(key_list[5], (NZ, NLAT, NLON), jnp.float32) ** block_scale(key_list[5], (NZ, NLAT, NLON), ((1, 16), (2, 32)), -0.2, 0.2)), 0.5, 8.0).astype(jnp.bfloat16),
    }


def operator(field, coef_east, coef_north, coef_down):
    value_east = jnp.roll(field, -1, axis=2)
    value_north = jnp.concatenate([field[:, 1:], jnp.zeros_like(field[:, :1])], axis=1)
    value_below = jnp.concatenate([field[1:], jnp.zeros_like(field[:1])], axis=0)
    flux_east = coef_east * (value_east - field)
    flux_north = coef_north * (value_north - field)
    flux_down = coef_down * (value_below - field)
    flux_west = jnp.roll(flux_east, 1, axis=2)
    flux_south = jnp.concatenate([jnp.zeros_like(flux_north[:, :1]), flux_north[:, :-1]], axis=1)
    flux_above = jnp.concatenate([jnp.zeros_like(flux_down[:1]), flux_down[:-1]], axis=0)
    return field + (flux_west - flux_east) + (flux_south - flux_north) + (flux_above - flux_down)


def reference(right_side, sea_mask, levels, east_diffusivity, north_diffusivity, vertical_diffusivity):
    depth_index = lax.broadcasted_iota(jnp.int32, sea_mask.shape, 0)
    ocean = ((sea_mask == 1) & (depth_index < levels[None])).astype(jnp.float32)
    ocean_east = jnp.roll(ocean, -1, axis=2)
    ocean_north = jnp.concatenate([ocean[:, 1:], jnp.zeros_like(ocean[:, :1])], axis=1)
    ocean_below = jnp.concatenate([ocean[1:], jnp.zeros_like(ocean[:1])], axis=0)
    coef_east = east_diffusivity.astype(jnp.float32) * ocean * ocean_east
    coef_north = north_diffusivity.astype(jnp.float32) * ocean * ocean_north
    coef_down = vertical_diffusivity.astype(jnp.float32) * ocean * ocean_below

    def solve_one(source):
        solution = jnp.zeros_like(source)
        residual = source
        direction = source
        norm_now = jnp.sum(residual * residual)
        for iteration in range(ITERS):
            image = operator(direction, coef_east, coef_north, coef_down)
            step_size = norm_now / jnp.sum(direction * image)
            solution = solution + step_size * direction
            residual = residual - step_size * image
            norm_next = jnp.sum(residual * residual)
            direction = residual + (norm_next / norm_now) * direction
            norm_now = norm_next
        return solution, residual

    solution_field, residual = lax.map(solve_one, right_side)
    return solution_field, residual
```

```python
import jax
import jax.numpy as jnp
from jax import lax
from jax.experimental import pallas as pl
from jax.experimental.pallas import tpu as pltpu
from jax.sharding import PartitionSpec as P

MESH = pl.DeviceIdType.MESH
HUB = 1
CHUNK = 4


def kernel(nlon, nlat, rhs, mask_in, levels_in, ed_in, nd_in, vd_in,
           w_out, z_out, coef0, coef1, coef2, coef3, coef4,
           bp, wp, maskv, levelsv, edv, ndv, vdv,
           ocp, edoc, ndp, ce, cw, cn, cs, cdp,
           col_out, col_in, wcol_out, wcol_in,
           row_out, row_in, crow_out, crow_in, wrow_out, wrow_in,
           part, hub_in, peer_in, total,
           in_sem, send_sem, recv_sem, hub_send, hub_recv):
    levels_n = mask_in.shape[0]
    rows = mask_in.shape[1]
    lanes = mask_in.shape[2]
    lon, lat = lax.axis_index("lon"), lax.axis_index("lat")
    east = {"lon": lax.rem(lon + 1, nlon)}
    west = {"lon": lax.rem(lon + nlon - 1, nlon)}
    north = {"lat": lax.rem(lat + 1, nlat)}
    south = {"lat": lax.rem(lat + nlat - 1, nlat)}
    is_hub = lat == HUB

    barrier = pltpu.get_barrier_semaphore()
    for target in (east, west, north, south):
        pl.semaphore_signal(barrier, 1, device_id=target, device_id_type=MESH)

    loads = [
        pltpu.make_async_copy(mask_in, maskv, in_sem.at[0]),
        pltpu.make_async_copy(levels_in, levelsv, in_sem.at[1]),
        pltpu.make_async_copy(ed_in, edv, in_sem.at[2]),
        pltpu.make_async_copy(nd_in, ndv, in_sem.at[3]),
        pltpu.make_async_copy(vd_in, vdv, in_sem.at[4]),
        pltpu.make_async_copy(rhs, bp.at[:, pl.ds(1, levels_n)], in_sem.at[5]),
    ]
    for load in loads:
        load.start()

    @pl.when(is_hub)
    def _():
        def tell_member(d, carry):
            pl.semaphore_signal(barrier, 1, device_id={"lat": lax.rem(lat + d, nlat)}, device_id_type=MESH)
            return carry

        lax.fori_loop(1, nlat, tell_member, 0)

        def tell_peer(d, carry):
            pl.semaphore_signal(barrier, 1, device_id={"lon": lax.rem(lon + d, nlon)}, device_id_type=MESH)
            return carry

        lax.fori_loop(1, nlon, tell_peer, 0)

    zero_plane = jnp.zeros((2, 1, rows, lanes), jnp.float32)
    bp[:, 0:1] = zero_plane
    bp[:, levels_n + 1:levels_n + 2] = zero_plane
    wp[:, 0:1] = zero_plane
    wp[:, levels_n + 1:levels_n + 2] = zero_plane
    ocp[levels_n:levels_n + 1] = zero_plane[0]
    cdp[0:1] = zero_plane[0]

    lane2 = lax.broadcasted_iota(jnp.int32, (rows, lanes), 1)
    row2 = lax.broadcasted_iota(jnp.int32, (rows, lanes), 0)
    first_lane, last_lane = lane2 == 0, lane2 == lanes - 1
    first_row, last_row = row2 == 0, row2 == rows - 1

    def pack(piece, at, place):
        shift = (place - at) % lanes
        return pltpu.roll(piece, shift, 1) if shift else piece

    loads[0].wait()
    loads[1].wait()
    for k in range(levels_n):
        ocp[k] = jnp.where((maskv[k] == 1) & (levelsv[...] > k), 1.0, 0.0)
    for load in loads[2:5]:
        load.wait()
    for k in range(levels_n):
        oc = ocp[k]
        edoc[k] = edv[k].astype(jnp.float32) * oc
        nd = ndv[k].astype(jnp.float32) * oc
        ndp[k] = nd
        cdp[k + 1] = vdv[k].astype(jnp.float32) * oc * ocp[k + 1]
        crow_out[0, k] = oc[0:1]
        crow_out[1, k] = nd[rows - 1:rows]
    loads[5].wait()

    first_col = jnp.zeros((rows, lanes), jnp.float32)
    last_col = jnp.zeros((rows, lanes), jnp.float32)
    for t in range(2):
        for k in range(levels_n):
            piece = bp[t, k + 1]
            place = t * levels_n + k
            here = lane2 == place
            first_col = jnp.where(here, pack(piece, 0, place), first_col)
            last_col = jnp.where(here, pack(piece, lanes - 1, place), last_col)
            row_out[0, t, k] = piece[0:1]
            row_out[1, t, k] = piece[rows - 1:rows]
    for k in range(levels_n):
        place = 2 * levels_n + k
        here = lane2 == place
        first_col = jnp.where(here, pack(ocp[k], 0, place), first_col)
        last_col = jnp.where(here, pack(edoc[k], lanes - 1, place), last_col)
    col_out[0] = first_col
    col_out[1] = last_col

    def send(source, target, slot, number, device):
        copy = pltpu.make_async_remote_copy(
            source.at[slot], target.at[slot], send_sem.at[number], recv_sem.at[number],
            device_id=device, device_id_type=MESH)
        copy.start()
        return copy

    pl.semaphore_wait(barrier, jnp.where(is_hub, nlon + 3, 5))

    first = [
        send(row_out, row_in, 0, 0, south),
        send(row_out, row_in, 1, 1, north),
        send(crow_out, crow_in, 0, 2, south),
        send(crow_out, crow_in, 1, 3, north),
        send(col_out, col_in, 0, 4, west),
        send(col_out, col_in, 1, 5, east),
    ]
    for copy in first:
        copy.wait()

    from_east, from_west = col_in[0], col_in[1]
    top = jnp.where(lat == nlat - 1, 0.0, 1.0)
    bottom = jnp.where(lat == 0, 0.0, 1.0)
    for k in range(levels_n):
        oc = ocp[k]
        place = 2 * levels_n + k
        ed, nd = edoc[k], ndp[k]
        oc_east = jnp.where(last_lane, pack(from_east, place, lanes - 1), pltpu.roll(oc, lanes - 1, 1))
        ed_west = jnp.where(first_lane, pack(from_west, place, 0), pltpu.roll(ed, 1, 1))
        oc_north = jnp.where(last_row, crow_in[0, k] * top, pltpu.roll(oc, rows - 1, 0))
        nd_south = jnp.where(first_row, crow_in[1, k] * bottom, pltpu.roll(nd, 1, 0))
        ce[k] = ed * oc_east
        cw[k] = ed_west * oc
        cn[k] = nd * oc_north
        cs[k] = nd_south * oc

    def sides(field, t, k, east_col, west_col, north_row, south_row):
        v = field[t, k + 1]
        place = t * levels_n + k
        v_east = jnp.where(last_lane, pack(east_col, place, lanes - 1), pltpu.roll(v, lanes - 1, 1))
        v_west = jnp.where(first_lane, pack(west_col, place, 0), pltpu.roll(v, 1, 1))
        v_north = jnp.where(last_row, north_row, pltpu.roll(v, rows - 1, 0))
        v_south = jnp.where(first_row, south_row, pltpu.roll(v, 1, 0))
        return v, v_east, v_west, v_north, v_south

    def diffuse(field, t, k, *halo):
        v, v_east, v_west, v_north, v_south = sides(field, t, k, *halo)
        return v, (
            (ce[k] * (v - v_east) + cw[k] * (v - v_west))
            + (cn[k] * (v - v_north) + cs[k] * (v - v_south))
            + (cdp[k + 1] * (v - field[t, k + 2]) + cdp[k] * (v - field[t, k]))
        )

    sums = []
    first_col = jnp.zeros((rows, lanes), jnp.float32)
    last_col = jnp.zeros((rows, lanes), jnp.float32)
    for t in range(2):
        s0 = s1 = s2 = jnp.zeros((rows, lanes), jnp.float32)
        for k in range(levels_n):
            v, w = diffuse(bp, t, k, from_east, from_west, row_in[0, t, k], row_in[1, t, k])
            wp[t, k + 1] = w
            w_out[t, k] = w
            s0, s1, s2 = s0 + v * v, s1 + v * w, s2 + w * w
            place = t * levels_n + k
            here = lane2 == place
            first_col = jnp.where(here, pack(w, 0, place), first_col)
            last_col = jnp.where(here, pack(w, lanes - 1, place), last_col)
            wrow_out[0, t, k] = w[0:1]
            wrow_out[1, t, k] = w[rows - 1:rows]
        sums.append([s0, s1, s2])
    wcol_out[0] = first_col
    wcol_out[1] = last_col
    second = [
        send(wrow_out, wrow_in, 0, 6, south),
        send(wrow_out, wrow_in, 1, 7, north),
        send(wcol_out, wcol_in, 0, 8, west),
        send(wcol_out, wcol_in, 1, 9, east),
    ]
    for copy in second:
        copy.wait()
    from_east, from_west = wcol_in[0], wcol_in[1]
    for t in range(2):
        s3 = jnp.zeros((rows, lanes), jnp.float32)
        for k in range(levels_n):
            w, z = diffuse(wp, t, k, from_east, from_west, wrow_in[0, t, k], wrow_in[1, t, k])
            z_out[t, k] = z
            s3 = s3 + w * z
        sums[t].append(s3)

    lane1 = lax.broadcasted_iota(jnp.int32, (1, lanes), 1)
    mine = jnp.zeros((1, lanes), jnp.float32)
    for t in range(2):
        for j in range(4):
            one = jnp.sum(jnp.sum(sums[t][j], axis=0, keepdims=True), axis=1, keepdims=True)
            mine = jnp.where(lane1 == t * 4 + j, one, mine)
    part[0] = mine

    @pl.when(jnp.logical_not(is_hub))
    def _():
        slot = lax.rem(lat - HUB + nlat, nlat)
        give = pltpu.make_async_remote_copy(
            part.at[0], hub_in.at[slot], hub_send.at[0], hub_recv.at[0],
            device_id={"lat": HUB}, device_id_type=MESH)
        give.start()
        give.wait_send()
        take = pltpu.make_async_copy(total.at[0], total.at[0], hub_recv.at[2])
        take.wait()

    @pl.when(is_hub)
    def _():
        members = hub_in.at[pl.ds(1, nlat - 1)]
        peers = peer_in.at[pl.ds(1, nlon - 1)]
        hub_in[0] = part[0]
        pltpu.make_async_copy(members, members, hub_recv.at[0]).wait()
        peer_in[0] = jnp.sum(hub_in[...], axis=0)

        def give_peer(d, carry):
            pltpu.make_async_remote_copy(
                peer_in.at[0], peer_in.at[d], hub_send.at[1], hub_recv.at[1],
                device_id={"lon": lax.rem(lon + d, nlon)}, device_id_type=MESH).start()
            return carry

        lax.fori_loop(1, nlon, give_peer, 0)
        pltpu.make_async_copy(peers, peers, hub_recv.at[1]).wait()
        total[0] = jnp.sum(peer_in[...], axis=0)

        def give_member(d, carry):
            pltpu.make_async_remote_copy(
                total.at[0], total.at[0], hub_send.at[2], hub_recv.at[2],
                device_id={"lat": lax.rem(lat + d, nlat)}, device_id_type=MESH).start()
            return carry

        lax.fori_loop(1, nlat, give_member, 0)
        pltpu.make_async_copy(peers, peers, hub_send.at[1]).wait()
        pltpu.make_async_copy(members, members, hub_send.at[2]).wait()

    got = total[0]
    for t in range(2):
        m0, l1, l2, l3 = [jnp.sum(jnp.where(lane1 == t * 4 + j, got, 0.0), axis=1, keepdims=True) for j in range(4)]
        c0 = l1 / m0
        a0 = m0 / (m0 + l1)
        spread = l2 - l1 * c0
        curve = l3 - c0 * (2.0 * l2 - c0 * l1)
        beta = a0 * a0 * spread / m0
        a1 = spread / (spread + curve - a0 * spread * (spread / m0))
        g = a0 * c0 + beta
        values = (a0 + a1 * g, -a1 * a0, a0 * c0 - a1 * g, a1 * a0 - a0 - a1 * g, a1 * a0)
        for coef, value in zip((coef0, coef1, coef2, coef3, coef4), values, strict=True):
            coef[t:t + 1] = jnp.broadcast_to(value, (1, lanes))


def solution(mesh):
    nlon, nlat = mesh.shape["lon"], mesh.shape["lat"]

    def body(rhs, sea_mask, levels, ed, nd, vd):
        tracers, nz, rows, lanes = rhs.shape
        field = (tracers, nz + 2, rows, lanes)
        block = (nz, rows, lanes)
        f32 = jnp.float32
        whole = pl.BlockSpec(memory_space=pltpu.VMEM)
        w, z, *coef = pl.pallas_call(
            lambda *refs: kernel(nlon, nlat, *refs),
            out_shape=(
                jax.ShapeDtypeStruct(rhs.shape, f32),
                jax.ShapeDtypeStruct(rhs.shape, f32),
            ) + (jax.ShapeDtypeStruct((tracers, lanes), f32),) * 5,
            in_specs=[pl.BlockSpec(memory_space=pltpu.HBM)] * 6,
            out_specs=(whole,) * 7,
            scratch_shapes=[
                pltpu.VMEM(field, f32), pltpu.VMEM(field, f32),
                pltpu.VMEM(block, jnp.int32), pltpu.VMEM((rows, lanes), jnp.int32),
                pltpu.VMEM(block, jnp.bfloat16), pltpu.VMEM(block, jnp.bfloat16), pltpu.VMEM(block, jnp.bfloat16),
                pltpu.VMEM((nz + 1, rows, lanes), f32), pltpu.VMEM(block, f32), pltpu.VMEM(block, f32),
                pltpu.VMEM(block, f32), pltpu.VMEM(block, f32), pltpu.VMEM(block, f32), pltpu.VMEM(block, f32),
                pltpu.VMEM((nz + 1, rows, lanes), f32),
                pltpu.VMEM((2, rows, lanes), f32), pltpu.VMEM((2, rows, lanes), f32),
                pltpu.VMEM((2, rows, lanes), f32), pltpu.VMEM((2, rows, lanes), f32),
                pltpu.VMEM((2, tracers, nz, 1, lanes), f32), pltpu.VMEM((2, tracers, nz, 1, lanes), f32),
                pltpu.VMEM((2, nz, 1, lanes), f32), pltpu.VMEM((2, nz, 1, lanes), f32),
                pltpu.VMEM((2, tracers, nz, 1, lanes), f32), pltpu.VMEM((2, tracers, nz, 1, lanes), f32),
                pltpu.VMEM((1, 1, lanes), f32), pltpu.VMEM((nlat, 1, lanes), f32),
                pltpu.VMEM((nlon, 1, lanes), f32), pltpu.VMEM((1, 1, lanes), f32),
                pltpu.SemaphoreType.DMA((6,)), pltpu.SemaphoreType.DMA((10,)), pltpu.SemaphoreType.DMA((10,)),
                pltpu.SemaphoreType.DMA((3,)), pltpu.SemaphoreType.DMA((3,)),
            ],
            compiler_params=pltpu.CompilerParams(collective_id=0, has_side_effects=True, vmem_limit_bytes=32 * 1024 * 1024),
        )(*[pltpu.with_memory_space_constraint(one, pltpu.HBM) for one in (rhs, sea_mask, levels, ed, nd, vd)])
        c = [one[:, None, None, :] for one in coef]
        return c[0] * rhs + c[1] * w, c[2] * rhs + c[3] * w + c[4] * z

    return jax.shard_map(
        body,
        mesh=mesh,
        in_specs=(
            P(None, None, "lat", "lon"),
            P(None, "lat", "lon"),
            P("lat", "lon"),
            P(None, "lat", "lon"),
            P(None, "lat", "lon"),
            P(None, "lat", "lon"),
        ),
        out_specs=(P(None, None, "lat", "lon"), P(None, None, "lat", "lon")),
        check_vma=False,
    )
```

```python
import jax
import jax.numpy as jnp
from jax import lax
from jax.experimental import pallas as pl
from jax.experimental.pallas import tpu as pltpu
from jax.sharding import PartitionSpec as P

MESH = pl.DeviceIdType.MESH
HUB = 1


def kernel(nlon, nlat, rhs, mask_in, levels_in, ed_in, nd_in, vd_in,
           w_out, z_out, coef0, coef1, coef2, coef3, coef4,
           bp, maskv, levelsv, edv, ndv, vdv,
           ocp, ce, cn, cd,
           col_out, from_east, from_west,
           row0_out, row15_out, from_north, from_south,
           corner_out, corner_in, wcol_out, wcol_west, wrow_out, wrow_south, zrow_north,
           part, hub_in, peer_in, total,
           in_sem, send_sem, recv_sem, hub_send, hub_recv):
    nz, rows, lanes = mask_in.shape
    lon, lat = lax.axis_index("lon"), lax.axis_index("lat")
    lon_east, lon_west = lax.rem(lon + 1, nlon), lax.rem(lon + nlon - 1, nlon)
    lat_north, lat_south = lax.rem(lat + 1, nlat), lax.rem(lat + nlat - 1, nlat)
    east, west = {"lon": lon_east}, {"lon": lon_west}
    north, south = {"lat": lat_north}, {"lat": lat_south}
    north_east = {"lon": lon_east, "lat": lat_north}
    north_west = {"lon": lon_west, "lat": lat_north}
    south_east = {"lon": lon_east, "lat": lat_south}
    south_west = {"lon": lon_west, "lat": lat_south}
    is_hub = lat == HUB

    barrier = pltpu.get_barrier_semaphore()
    for target in (east, west, north, south, north_east, north_west, south_east):
        pl.semaphore_signal(barrier, 1, device_id=target, device_id_type=MESH)

    loads = [
        pltpu.make_async_copy(mask_in, maskv, in_sem.at[0]),
        pltpu.make_async_copy(levels_in, levelsv, in_sem.at[1]),
        pltpu.make_async_copy(ed_in, edv, in_sem.at[2]),
        pltpu.make_async_copy(nd_in, ndv, in_sem.at[3]),
        pltpu.make_async_copy(vd_in, vdv, in_sem.at[4]),
        pltpu.make_async_copy(rhs, bp, in_sem.at[5]),
    ]
    for load in loads:
        load.start()

    @pl.when(is_hub)
    def _():
        def tell_member(d, carry):
            pl.semaphore_signal(barrier, 1, device_id={"lat": lax.rem(lat + d, nlat)}, device_id_type=MESH)
            return carry

        lax.fori_loop(1, nlat, tell_member, 0)

        def tell_peer(d, carry):
            pl.semaphore_signal(barrier, 1, device_id={"lon": lax.rem(lon + d, nlon)}, device_id_type=MESH)
            return carry

        lax.fori_loop(1, nlon, tell_peer, 0)

    lane2 = lax.broadcasted_iota(jnp.int32, (rows, lanes), 1)
    row2 = lax.broadcasted_iota(jnp.int32, (rows, lanes), 0)
    lane1 = lax.broadcasted_iota(jnp.int32, (1, lanes), 1)
    first_row, last_row = row2 == 0, row2 == rows - 1
    edge_lane, edge_lane1 = (lane2 == 0) | (lane2 == lanes - 1), (lane1 == 0) | (lane1 == lanes - 1)
    pair = lane2 // 2
    even, even1 = lane2 % 2 == 0, lane1 % 2 == 0
    zero = jnp.zeros((rows, lanes), jnp.float32)

    def turn(piece, shift, axis=1):
        shift = shift % piece.shape[axis]
        return pltpu.roll(piece, shift, axis) if shift else piece

    def pack(piece, j, into):
        return jnp.where(pair == j, turn(piece, 2 * j + 1), into)

    def unpack(packed, j):
        return jnp.where(edge_lane, turn(packed, -1 - 2 * j), 0.0)

    def facing(east_packed, west_packed):
        return jnp.where(even if east_packed.shape[0] == rows else even1, turn(east_packed, -1), turn(west_packed, 1))

    def both(packed):
        return packed + turn(packed, 2 * nz)

    loads[0].wait()
    loads[1].wait()
    for k in range(nz):
        ocp[k] = jnp.where((maskv[k] == 1) & (levelsv[...] > k), 1.0, 0.0)
    for load in loads[2:5]:
        load.wait()
    half_lane = lane2 < lanes - 1
    edge_coef, edge_nd = zero, zero
    for k in range(nz):
        oc = ocp[k]
        ed = edv[k].astype(jnp.float32) * oc
        nd = ndv[k].astype(jnp.float32) * oc
        ce[k] = jnp.where(half_lane, ed * turn(oc, -1), 0.0)
        cn[k] = jnp.where(last_row, 0.0, nd * turn(oc, -1, 0))
        if k < nz - 1:
            cd[k] = vdv[k].astype(jnp.float32) * oc * ocp[k + 1]
        row0_out[2, k] = oc[0:1]
        row15_out[2, k] = nd[rows - 1:rows]
        edge_coef = jnp.where(pair == k, jnp.where(even, turn(ed, 2 * k + 1), turn(oc, 2 * k + 1)), edge_coef)
        edge_nd = pack(nd, k, edge_nd)
    edge_coef, edge_nd = both(edge_coef), both(edge_nd)
    loads[5].wait()

    sums = []
    edge_b, edge_p = zero, zero
    for t in range(2):
        s0 = zero
        down_above = zero
        for k in range(nz):
            v = bp[t, k]
            flow_east = ce[k] * (v - turn(v, -1))
            flow_north = cn[k] * (v - turn(v, -1, 0))
            inner = (flow_east - turn(flow_east, 1)) + (flow_north - turn(flow_north, 1, 0))
            if k < nz - 1:
                down = cd[k] * (v - bp[t, k + 1])
                inner = inner + (down - down_above)
                down_above = down
            else:
                inner = inner - down_above
            w_out[t, k] = inner
            s0 = s0 + v * v
            j = t * nz + k
            edge_b, edge_p = pack(v, j, edge_b), pack(inner, j, edge_p)
            row0_out[t, k] = v[0:1]
            row0_out[3 + t, k] = inner[0:1]
            row15_out[t, k] = v[rows - 1:rows]
        sums.append([s0])
    col_out[0], col_out[1], col_out[2], col_out[3] = edge_b, edge_coef, edge_p, edge_nd
    corner_out[0, 0], corner_out[0, 1] = edge_b[0:1], edge_coef[0:1]
    corner_out[1, 0], corner_out[1, 1] = edge_b[rows - 1:rows], edge_nd[rows - 1:rows]

    pl.semaphore_wait(barrier, jnp.where(is_hub, nlon + 6, 8))

    def send(source, target, number, device):
        copy = pltpu.make_async_remote_copy(
            source, target, send_sem.at[number], recv_sem.at[number], device_id=device, device_id_type=MESH)
        copy.start()
        return copy

    halo = [
        send(col_out, from_east, 0, west),
        send(col_out.at[pl.ds(0, 2)], from_west, 1, east),
        send(corner_out.at[0], corner_in.at[1], 2, south_west),
        send(corner_out.at[0], corner_in.at[2], 3, south_east),
        send(corner_out.at[1], corner_in.at[3], 4, north_west),
        send(corner_out.at[0], corner_in.at[0], 5, south),
        send(row0_out, from_north, 6, south),
        send(row15_out, from_south, 7, north),
    ]
    for copy in halo:
        copy.wait()

    top = jnp.where(lat == nlat - 1, 0.0, 1.0)
    bottom = jnp.where(lat == 0, 0.0, 1.0)
    cross = edge_coef * facing(from_east[1], from_west[1])
    faced_b = facing(from_east[0], from_west[0])
    flow = cross * (edge_b - faced_b)
    ghost = turn(from_east[2], -1) - flow
    ne_b, ne_oc = turn(corner_in[1, 0], -1), turn(corner_in[1, 1], -1)
    se_b, se_nd = turn(corner_in[3, 0], -1), turn(corner_in[3, 1], -1)
    east_oc, east_nd = turn(from_east[1], -1), turn(from_east[3], -1)
    ghost = ghost + jnp.where(last_row, (east_nd * (ne_oc * top)) * (faced_b - ne_b), 0.0)
    ghost = ghost + jnp.where(first_row, (east_oc * (se_nd * bottom)) * (faced_b - se_b), 0.0)
    flow_ghost = (corner_in[0, 1] * facing(corner_in[1, 1], corner_in[2, 1])) * (
        corner_in[0, 0] - facing(corner_in[1, 0], corner_in[2, 0]))

    edge_w = zero
    for t in range(2):
        s1 = s2 = s3 = zero
        s3_row = jnp.zeros((1, lanes), jnp.float32)
        w_above = None
        for k in range(nz):
            v = bp[t, k]
            j = t * nz + k
            c_north = row15_out[2, k] * (from_north[2, k] * top)
            c_south = (from_south[2, k] * bottom) * row0_out[2, k]
            out_north = c_north * (row15_out[t, k] - from_north[t, k])
            out_south = c_south * (row0_out[t, k] - from_south[t, k])
            w = w_out[t, k] + unpack(flow, j)
            w = w + jnp.where(last_row, out_north, jnp.where(first_row, out_south, 0.0))
            w_out[t, k] = w
            s1, s2 = s1 + v * w, s2 + w * w
            gap_east, gap_north = w - turn(w, -1), w - turn(w, -1, 0)
            s3 = s3 + (ce[k] * gap_east) * gap_east + (cn[k] * gap_north) * gap_north
            if k > 0:
                gap_down = w_above - w
                s3 = s3 + (cd[k - 1] * gap_down) * gap_down
            w_above = w
            edge_w = pack(w, j, edge_w)
            w_north = from_north[3 + t, k] - out_north + jnp.where(edge_lane1, turn(flow_ghost, -1 - 2 * j), 0.0)
            gap = w[rows - 1:rows] - w_north
            out_north = c_north * gap
            zrow_north[t, k] = out_north
            s3_row = s3_row + out_north * gap
            wrow_out[t, k] = w[rows - 1:rows]
        sums[t] += [s1, s2, s3 + jnp.where(first_row, s3_row, 0.0)]
    wcol_out[...] = edge_w
    later = [
        send(wcol_out, wcol_west, 8, east),
        send(wrow_out, wrow_south, 9, north),
    ]
    gap = edge_w - ghost
    east_sum = jnp.where(even, (cross * gap) * gap, 0.0)
    for t in range(2):
        sums[t][3] = sums[t][3] + jnp.where(lane2 // (2 * nz) == t, east_sum, 0.0)

    mine = jnp.zeros((1, lanes), jnp.float32)
    for t in range(2):
        for j in range(4):
            one = jnp.sum(jnp.sum(sums[t][j], axis=0, keepdims=True), axis=1, keepdims=True)
            mine = jnp.where(lane1 == t * 4 + j, one, mine)
    part[0] = mine

    @pl.when(jnp.logical_not(is_hub))
    def _():
        slot = lax.rem(lat - HUB + nlat, nlat)
        give = pltpu.make_async_remote_copy(
            part.at[0], hub_in.at[slot], hub_send.at[0], hub_recv.at[0],
            device_id={"lat": HUB}, device_id_type=MESH)
        give.start()
        give.wait_send()
    for copy in later:
        copy.wait()
    flow = cross * (edge_w - jnp.where(even, ghost, turn(wcol_west[...], 1)))
    for t in range(2):
        down_above = zero
        for k in range(nz):
            w = w_out[t, k]
            j = t * nz + k
            c_south = (from_south[2, k] * bottom) * row0_out[2, k]
            out_south = c_south * (w[0:1] - wrow_south[t, k])
            flow_east = ce[k] * (w - turn(w, -1))
            flow_north = cn[k] * (w - turn(w, -1, 0))
            z = (flow_east - turn(flow_east, 1)) + (flow_north - turn(flow_north, 1, 0))
            if k < nz - 1:
                down = cd[k] * (w - w_out[t, k + 1])
                z = z + (down - down_above)
                down_above = down
            else:
                z = z - down_above
            z = z + unpack(flow, j)
            z_out[t, k] = z + jnp.where(last_row, zrow_north[t, k], jnp.where(first_row, out_south, 0.0))

    @pl.when(jnp.logical_not(is_hub))
    def _():
        pltpu.make_async_copy(total.at[0], total.at[0], hub_recv.at[2]).wait()

    @pl.when(is_hub)
    def _():
        members = hub_in.at[pl.ds(1, nlat - 1)]
        peers = peer_in.at[pl.ds(1, nlon - 1)]
        hub_in[0] = part[0]
        pltpu.make_async_copy(members, members, hub_recv.at[0]).wait()
        peer_in[0] = jnp.sum(hub_in[...], axis=0)

        def give_peer(d, carry):
            pltpu.make_async_remote_copy(
                peer_in.at[0], peer_in.at[d], hub_send.at[1], hub_recv.at[1],
                device_id={"lon": lax.rem(lon + d, nlon)}, device_id_type=MESH).start()
            return carry

        lax.fori_loop(1, nlon, give_peer, 0)
        pltpu.make_async_copy(peers, peers, hub_recv.at[1]).wait()
        total[0] = jnp.sum(peer_in[...], axis=0)

        def give_member(d, carry):
            pltpu.make_async_remote_copy(
                total.at[0], total.at[0], hub_send.at[2], hub_recv.at[2],
                device_id={"lat": lax.rem(lat + d, nlat)}, device_id_type=MESH).start()
            return carry

        lax.fori_loop(1, nlat, give_member, 0)
        pltpu.make_async_copy(peers, peers, hub_send.at[1]).wait()
        pltpu.make_async_copy(members, members, hub_send.at[2]).wait()

    got = total[0]
    for t in range(2):
        m0, l1, l2, l3 = [jnp.sum(jnp.where(lane1 == t * 4 + j, got, 0.0), axis=1, keepdims=True) for j in range(4)]
        c0 = l1 / m0
        a0 = m0 / (m0 + l1)
        spread = l2 - l1 * c0
        curve = l3 - c0 * (2.0 * l2 - c0 * l1)
        beta = a0 * a0 * spread / m0
        a1 = spread / (spread + curve - a0 * spread * (spread / m0))
        g = a0 * c0 + beta
        values = (a0 + a1 * g, -a1 * a0, a0 * c0 - a1 * g, a1 * a0 - a0 - a1 * g, a1 * a0)
        for coef, value in zip((coef0, coef1, coef2, coef3, coef4), values, strict=True):
            coef[t:t + 1] = jnp.broadcast_to(value, (1, lanes))


def solution(mesh):
    nlon, nlat = mesh.shape["lon"], mesh.shape["lat"]

    def body(rhs, sea_mask, levels, ed, nd, vd):
        tracers, nz, rows, lanes = rhs.shape
        block = (nz, rows, lanes)
        f32 = jnp.float32
        whole = pl.BlockSpec(memory_space=pltpu.VMEM)
        w, z, *coef = pl.pallas_call(
            lambda *refs: kernel(nlon, nlat, *refs),
            out_shape=(
                jax.ShapeDtypeStruct(rhs.shape, f32),
                jax.ShapeDtypeStruct(rhs.shape, f32),
            ) + (jax.ShapeDtypeStruct((tracers, lanes), f32),) * 5,
            in_specs=[pl.BlockSpec(memory_space=pltpu.HBM)] * 6,
            out_specs=(whole,) * 7,
            scratch_shapes=[
                pltpu.VMEM(rhs.shape, f32),
                pltpu.VMEM(block, jnp.int32), pltpu.VMEM((rows, lanes), jnp.int32),
                pltpu.VMEM(block, jnp.bfloat16), pltpu.VMEM(block, jnp.bfloat16), pltpu.VMEM(block, jnp.bfloat16),
                pltpu.VMEM(block, f32),
                pltpu.VMEM(block, f32), pltpu.VMEM(block, f32), pltpu.VMEM(block, f32),
                pltpu.VMEM((4, rows, lanes), f32), pltpu.VMEM((4, rows, lanes), f32), pltpu.VMEM((2, rows, lanes), f32),
                pltpu.VMEM((5, nz, 1, lanes), f32), pltpu.VMEM((3, nz, 1, lanes), f32),
                pltpu.VMEM((5, nz, 1, lanes), f32), pltpu.VMEM((3, nz, 1, lanes), f32),
                pltpu.VMEM((2, 2, 1, lanes), f32), pltpu.VMEM((4, 2, 1, lanes), f32),
                pltpu.VMEM((rows, lanes), f32), pltpu.VMEM((rows, lanes), f32),
                pltpu.VMEM((2, nz, 1, lanes), f32), pltpu.VMEM((2, nz, 1, lanes), f32), pltpu.VMEM((2, nz, 1, lanes), f32),
                pltpu.VMEM((1, 1, lanes), f32), pltpu.VMEM((nlat, 1, lanes), f32),
                pltpu.VMEM((nlon, 1, lanes), f32), pltpu.VMEM((1, 1, lanes), f32),
                pltpu.SemaphoreType.DMA((6,)), pltpu.SemaphoreType.DMA((10,)), pltpu.SemaphoreType.DMA((10,)),
                pltpu.SemaphoreType.DMA((3,)), pltpu.SemaphoreType.DMA((3,)),
            ],
            compiler_params=pltpu.CompilerParams(collective_id=0, has_side_effects=True, vmem_limit_bytes=32 * 1024 * 1024),
        )(*[pltpu.with_memory_space_constraint(one, pltpu.HBM) for one in (rhs, sea_mask, levels, ed, nd, vd)])
        c = [one[:, None, None, :] for one in coef]
        return c[0] * rhs + c[1] * w, c[2] * rhs + c[3] * w + c[4] * z

    return jax.shard_map(
        body,
        mesh=mesh,
        in_specs=(
            P(None, None, "lat", "lon"),
            P(None, "lat", "lon"),
            P("lat", "lon"),
            P(None, "lat", "lon"),
            P(None, "lat", "lon"),
            P(None, "lat", "lon"),
        ),
        out_specs=(P(None, None, "lat", "lon"), P(None, None, "lat", "lon")),
        check_vma=False,
    )
```

```python
import jax
import jax.numpy as jnp
from jax import lax
from jax.experimental import pallas as pl
from jax.experimental.pallas import tpu as pltpu
from jax.sharding import PartitionSpec as P

MESH = pl.DeviceIdType.MESH
UNROLL = 4
HUB = 1


def kernel(nlon, nlat, rhs, mask_in, levels_in, ed_in, nd_in, vd_in,
           w_out, z_out, coef0, coef1, coef2, coef3, coef4,
           bp, maskv, levelsv, edv, ndv, vdv,
           ocp, edp, ndp, ce, cw, cn, cs, cd,
           col_out, from_east, from_west,
           row0_out, row15_out, from_north, from_south,
           corner_out, corner_in, wcol_out, wcol_west, wrow_out, wrow_south, zrow_north,
           part, hub_in, peer_in, total,
           in_sem, send_sem, recv_sem, hub_send, hub_recv):
    rows, lanes = levels_in.shape
    nz = mask_in.shape[0] // rows
    lon, lat = lax.axis_index("lon"), lax.axis_index("lat")
    lon_east, lon_west = lax.rem(lon + 1, nlon), lax.rem(lon + nlon - 1, nlon)
    lat_north, lat_south = lax.rem(lat + 1, nlat), lax.rem(lat + nlat - 1, nlat)
    east, west = {"lon": lon_east}, {"lon": lon_west}
    north, south = {"lat": lat_north}, {"lat": lat_south}
    north_east = {"lon": lon_east, "lat": lat_north}
    north_west = {"lon": lon_west, "lat": lat_north}
    south_east = {"lon": lon_east, "lat": lat_south}
    south_west = {"lon": lon_west, "lat": lat_south}
    is_hub = lat == HUB

    barrier = pltpu.get_barrier_semaphore()
    for target in (east, west, north, south, north_east, north_west, south_east):
        pl.semaphore_signal(barrier, 1, device_id=target, device_id_type=MESH)

    loads = [
        pltpu.make_async_copy(mask_in, maskv, in_sem.at[0]),
        pltpu.make_async_copy(levels_in, levelsv, in_sem.at[1]),
        pltpu.make_async_copy(ed_in, edv, in_sem.at[2]),
        pltpu.make_async_copy(nd_in, ndv, in_sem.at[3]),
        pltpu.make_async_copy(vd_in, vdv, in_sem.at[4]),
        pltpu.make_async_copy(rhs, bp, in_sem.at[5]),
    ]
    for load in loads:
        load.start()

    @pl.when(is_hub)
    def _():
        def tell_member(d, carry):
            pl.semaphore_signal(barrier, 1, device_id={"lat": lax.rem(lat + d, nlat)}, device_id_type=MESH)
            return carry

        lax.fori_loop(1, nlat, tell_member, 0)

        def tell_peer(d, carry):
            pl.semaphore_signal(barrier, 1, device_id={"lon": lax.rem(lon + d, nlon)}, device_id_type=MESH)
            return carry

        lax.fori_loop(1, nlon, tell_peer, 0)

    lane2 = lax.broadcasted_iota(jnp.int32, (rows, lanes), 1)
    row2 = lax.broadcasted_iota(jnp.int32, (rows, lanes), 0)
    lane1 = lax.broadcasted_iota(jnp.int32, (1, lanes), 1)
    lane_z = lax.broadcasted_iota(jnp.int32, (nz, lanes), 1)
    row_z = lax.broadcasted_iota(jnp.int32, (nz, lanes), 0)
    first_row, last_row = row2 == 0, row2 == rows - 1
    first_lane, last_lane = lane2 == 0, lane2 == lanes - 1
    edge_lane = first_lane | last_lane
    pair = lane2 // 2
    even, even1 = lane2 % 2 == 0, lane1 % 2 == 0
    zero = jnp.zeros((rows, lanes), jnp.float32)

    def at(k):
        return pl.ds(pl.multiple_of(k * rows, rows), rows)

    def over_levels(step, carry=0):
        def several(n, carry):
            for i in range(UNROLL):
                carry = step(n * UNROLL + i, carry)
            return carry

        return lax.fori_loop(0, nz // UNROLL, several, carry)

    row0, row15 = pl.ds(0, nz, stride=rows), pl.ds(rows - 1, nz, stride=rows)

    def turn(piece, shift, axis=1):
        if isinstance(shift, int):
            shift = shift % piece.shape[axis]
        return pltpu.roll(piece, shift, axis)

    def pack(piece, j, into):
        return jnp.where(pair == j, turn(piece, 2 * j + 1), into)

    def unpack(packed, j):
        return jnp.where(edge_lane, turn(packed, lanes - 1 - 2 * j), 0.0)

    def facing(east_packed, west_packed):
        return jnp.where(even if east_packed.shape[0] == rows else even1, turn(east_packed, -1), turn(west_packed, 1))

    def both(packed):
        return packed + turn(packed, 2 * nz)

    def inside(field, t, k):
        v = field[t, at(k)]
        flows = (ce[at(k)] * (v - turn(v, -1)) + cw[at(k)] * (v - turn(v, 1))) + (
            cn[at(k)] * (v - turn(v, -1, 0)) + cs[at(k)] * (v - turn(v, 1, 0)))
        below, above = field[t, at(jnp.minimum(k + 1, nz - 1))], field[t, at(jnp.maximum(k - 1, 0))]
        return v, flows + (cd[at(k + 1)] * (v - below) + cd[at(k)] * (v - above))

    loads[0].wait()
    loads[1].wait()
    @over_levels
    def _(k, carry):
        ocp[at(k)] = jnp.where((maskv[at(k)] == 1) & (levelsv[...] > k), 1.0, 0.0)
        return carry

    ocp[at(nz)] = zero
    cd[at(0)] = zero
    for load in loads[2:5]:
        load.wait()

    @over_levels
    def _(k, carry):
        oc = ocp[at(k)]
        edp[at(k)] = edv[at(k)].astype(jnp.float32) * oc
        ndp[at(k)] = ndv[at(k)].astype(jnp.float32) * oc
        cd[at(k + 1)] = vdv[at(k)].astype(jnp.float32) * oc * ocp[at(k + 1)]
        return carry

    def faces(k, carry):
        edge_coef, edge_nd = carry
        oc, ed, nd = ocp[at(k)], edp[at(k)], ndp[at(k)]
        ce[at(k)] = jnp.where(last_lane, 0.0, ed * turn(oc, -1))
        cw[at(k)] = jnp.where(first_lane, 0.0, turn(ed, 1) * oc)
        cn[at(k)] = jnp.where(last_row, 0.0, nd * turn(oc, -1, 0))
        cs[at(k)] = jnp.where(first_row, 0.0, turn(nd, 1, 0) * oc)
        return pack(jnp.where(last_lane, ed, oc), k, edge_coef), pack(nd, k, edge_nd)

    edge_coef, edge_nd = over_levels(faces, (zero, zero))
    edge_coef, edge_nd = both(edge_coef), both(edge_nd)
    row0_out[2] = ocp[row0]
    row15_out[2] = ndp[row15]
    loads[5].wait()

    def inner(k, carry):
        edge_b, edge_p, *squares = carry
        for t in range(2):
            v, flows = inside(bp, t, k)
            w_out[t, at(k)] = flows
            squares[t] = squares[t] + v * v
            j = t * nz + k
            edge_b, edge_p = pack(v, j, edge_b), pack(flows, j, edge_p)
        return edge_b, edge_p, *squares

    edge_b, edge_p, *squares = over_levels(inner, (zero,) * 4)
    sums = [[one] for one in squares]
    for t in range(2):
        row0_out[t] = bp[t, row0]
        row15_out[t] = bp[t, row15]
        row0_out[3 + t] = w_out[t, row0]
    col_out[0], col_out[1], col_out[2], col_out[3] = edge_b, edge_coef, edge_p, edge_nd
    corner_out[0, 0], corner_out[0, 1] = edge_b[0:1], edge_coef[0:1]
    corner_out[1, 0], corner_out[1, 1] = edge_b[rows - 1:rows], edge_nd[rows - 1:rows]

    pl.semaphore_wait(barrier, jnp.where(is_hub, nlon + 6, 8))

    def send(source, target, number, device):
        copy = pltpu.make_async_remote_copy(
            source, target, send_sem.at[number], recv_sem.at[number], device_id=device, device_id_type=MESH)
        copy.start()
        return copy

    halo = [
        send(col_out, from_east, 0, west),
        send(col_out.at[pl.ds(0, 2)], from_west, 1, east),
        send(corner_out.at[0], corner_in.at[1], 2, south_west),
        send(corner_out.at[0], corner_in.at[2], 3, south_east),
        send(corner_out.at[1], corner_in.at[3], 4, north_west),
        send(corner_out.at[0], corner_in.at[0], 5, south),
        send(row0_out, from_north, 6, south),
        send(row15_out, from_south, 7, north),
    ]
    for copy in halo:
        copy.wait()

    top = jnp.where(lat == nlat - 1, 0.0, 1.0)
    bottom = jnp.where(lat == 0, 0.0, 1.0)
    cross = edge_coef * facing(from_east[1], from_west[1])
    faced_b = facing(from_east[0], from_west[0])
    flow = cross * (edge_b - faced_b)
    ghost = turn(from_east[2], -1) - flow
    ne_b, ne_oc = turn(corner_in[1, 0], -1), turn(corner_in[1, 1], -1)
    se_b, se_nd = turn(corner_in[3, 0], -1), turn(corner_in[3, 1], -1)
    east_oc, east_nd = turn(from_east[1], -1), turn(from_east[3], -1)
    ghost = ghost + jnp.where(last_row, (east_nd * (ne_oc * top)) * (faced_b - ne_b), 0.0)
    ghost = ghost + jnp.where(first_row, (east_oc * (se_nd * bottom)) * (faced_b - se_b), 0.0)
    flow_ghost = (corner_in[0, 1] * facing(corner_in[1, 1], corner_in[2, 1])) * (
        corner_in[0, 0] - facing(corner_in[1, 0], corner_in[2, 0]))
    c_north = row15_out[2] * (from_north[2] * top)
    c_south = (from_south[2] * bottom) * row0_out[2]
    north_ghost = []
    for t in range(2):
        out_north = c_north * (row15_out[t] - from_north[t])
        w_out[t, row15] = w_out[t, row15] + out_north
        w_out[t, row0] = w_out[t, row0] + c_south * (row0_out[t] - from_south[t])
        place = 2 * (t * nz + row_z)
        spread_ghost = jnp.broadcast_to(flow_ghost, (nz, lanes))
        east_end = jnp.sum(jnp.where(lane_z == place, spread_ghost, 0.0), axis=1, keepdims=True)
        west_end = jnp.sum(jnp.where(lane_z == place + 1, spread_ghost, 0.0), axis=1, keepdims=True)
        ends = jnp.where(lane_z == lanes - 1, east_end, jnp.where(lane_z == 0, west_end, 0.0))
        north_ghost.append(from_north[3 + t] - out_north + ends)

    def complete(k, carry):
        edge_w, *dots = carry
        for t in range(2):
            v = bp[t, at(k)]
            j = t * nz + k
            w = w_out[t, at(k)] + unpack(flow, j)
            w_out[t, at(k)] = w
            dots[2 * t], dots[2 * t + 1] = dots[2 * t] + v * w, dots[2 * t + 1] + w * w
            edge_w = pack(w, j, edge_w)
        return edge_w, *dots

    edge_w, *dots = over_levels(complete, (zero,) * 5)
    for t in range(2):
        sums[t] += dots[2 * t:2 * t + 2]
        wrow_out[t] = w_out[t, row15]
    wcol_out[...] = edge_w
    later = [
        send(wcol_out, wcol_west, 8, east),
        send(wrow_out, wrow_south, 9, north),
    ]
    gap = edge_w - ghost
    east_sum = jnp.where(even, (cross * gap) * gap, 0.0)

    def energy(k, carry):
        carry = list(carry)
        for t in range(2):
            w = w_out[t, at(k)]
            gap_east, gap_north = w - turn(w, -1), w - turn(w, -1, 0)
            gap_down = w - w_out[t, at(jnp.minimum(k + 1, nz - 1))]
            carry[t] = carry[t] + (((ce[at(k)] * gap_east) * gap_east + (cn[at(k)] * gap_north) * gap_north)
                                   + (cd[at(k + 1)] * gap_down) * gap_down)
        return tuple(carry)

    cubes = over_levels(energy, tuple(jnp.where(lane2 // (2 * nz) == t, east_sum, 0.0) for t in range(2)))
    for t in range(2):
        s3 = cubes[t]
        gap = wrow_out[t] - north_ghost[t]
        out_north = c_north * gap
        zrow_north[t] = out_north
        row_sum = out_north * gap
        for k in range(nz // rows):
            s3 = s3 + row_sum[k * rows:(k + 1) * rows]
        sums[t].append(s3)

    mine = jnp.zeros((rows // 2, lanes), jnp.float32)
    for t in range(2):
        for j in range(4):
            one = jnp.sum(sums[t][j][:rows // 2] + sums[t][j][rows // 2:], axis=1, keepdims=True)
            mine = jnp.where(lane2[:rows // 2] == t * 4 + j, one, mine)
    mine = jnp.sum(mine, axis=0, keepdims=True)
    part[0] = mine

    @pl.when(jnp.logical_not(is_hub))
    def _():
        slot = lax.rem(lat - HUB + nlat, nlat)
        give = pltpu.make_async_remote_copy(
            part.at[0], hub_in.at[slot], hub_send.at[0], hub_recv.at[0],
            device_id={"lat": HUB}, device_id_type=MESH)
        give.start()
        give.wait_send()
    for copy in later:
        copy.wait()
    flow = cross * (edge_w - jnp.where(even, ghost, turn(wcol_west[...], 1)))

    @over_levels
    def _(k, carry):
        for t in range(2):
            z_out[t, at(k)] = inside(w_out, t, k)[1] + unpack(flow, t * nz + k)
        return carry

    for t in range(2):
        z_out[t, row15] = z_out[t, row15] + zrow_north[t]
        z_out[t, row0] = z_out[t, row0] + c_south * (w_out[t, row0] - wrow_south[t])

    @pl.when(jnp.logical_not(is_hub))
    def _():
        pltpu.make_async_copy(total.at[0], total.at[0], hub_recv.at[2]).wait()

    @pl.when(is_hub)
    def _():
        members = hub_in.at[pl.ds(1, nlat - 1)]
        peers = peer_in.at[pl.ds(1, nlon - 1)]
        hub_in[0] = part[0]
        pltpu.make_async_copy(members, members, hub_recv.at[0]).wait()
        peer_in[0] = jnp.sum(hub_in[...], axis=0)

        def give_peer(d, carry):
            pltpu.make_async_remote_copy(
                peer_in.at[0], peer_in.at[d], hub_send.at[1], hub_recv.at[1],
                device_id={"lon": lax.rem(lon + d, nlon)}, device_id_type=MESH).start()
            return carry

        lax.fori_loop(1, nlon, give_peer, 0)
        pltpu.make_async_copy(peers, peers, hub_recv.at[1]).wait()
        total[0] = jnp.sum(peer_in[...], axis=0)

        def give_member(d, carry):
            pltpu.make_async_remote_copy(
                total.at[0], total.at[0], hub_send.at[2], hub_recv.at[2],
                device_id={"lat": lax.rem(lat + d, nlat)}, device_id_type=MESH).start()
            return carry

        lax.fori_loop(1, nlat, give_member, 0)

    got = total[0]
    for t in range(2):
        m0, l1, l2, l3 = [jnp.sum(jnp.where(lane1 == t * 4 + j, got, 0.0), axis=1, keepdims=True) for j in range(4)]
        c0 = l1 / m0
        a0 = m0 / (m0 + l1)
        spread = l2 - l1 * c0
        curve = l3 - c0 * (2.0 * l2 - c0 * l1)
        beta = a0 * a0 * spread / m0
        a1 = spread / (spread + curve - a0 * spread * (spread / m0))
        g = a0 * c0 + beta
        values = (a0 + a1 * g, -a1 * a0, a0 * c0 - a1 * g, a1 * a0 - a0 - a1 * g, a1 * a0)
        for coef, value in zip((coef0, coef1, coef2, coef3, coef4), values, strict=True):
            coef[t:t + 1] = jnp.broadcast_to(value, (1, lanes))

    @pl.when(is_hub)
    def _():
        peers, members = peer_in.at[pl.ds(1, nlon - 1)], hub_in.at[pl.ds(1, nlat - 1)]
        pltpu.make_async_copy(peers, peers, hub_send.at[1]).wait()
        pltpu.make_async_copy(members, members, hub_send.at[2]).wait()


def solution(mesh):
    nlon, nlat = mesh.shape["lon"], mesh.shape["lat"]

    def body(rhs, sea_mask, levels, ed, nd, vd):
        tracers, nz, rows, lanes = rhs.shape
        field, block = (tracers, nz * rows, lanes), (nz * rows, lanes)
        taller = ((nz + 1) * rows, lanes)
        flat = [rhs.reshape(field), sea_mask.reshape(block), levels] + [one.reshape(block) for one in (ed, nd, vd)]
        f32 = jnp.float32
        whole = pl.BlockSpec(memory_space=pltpu.VMEM)
        w, z, *coef = pl.pallas_call(
            lambda *refs: kernel(nlon, nlat, *refs),
            out_shape=(
                jax.ShapeDtypeStruct(field, f32),
                jax.ShapeDtypeStruct(field, f32),
            ) + (jax.ShapeDtypeStruct((tracers, lanes), f32),) * 5,
            in_specs=[pl.BlockSpec(memory_space=pltpu.HBM)] * 6,
            out_specs=(whole,) * 7,
            scratch_shapes=[
                pltpu.VMEM(field, f32),
                pltpu.VMEM(block, jnp.int32), pltpu.VMEM((rows, lanes), jnp.int32),
                pltpu.VMEM(block, jnp.bfloat16), pltpu.VMEM(block, jnp.bfloat16), pltpu.VMEM(block, jnp.bfloat16),
                pltpu.VMEM(taller, f32), pltpu.VMEM(block, f32), pltpu.VMEM(block, f32),
                pltpu.VMEM(block, f32), pltpu.VMEM(block, f32), pltpu.VMEM(block, f32), pltpu.VMEM(block, f32),
                pltpu.VMEM(taller, f32),
                pltpu.VMEM((4, rows, lanes), f32), pltpu.VMEM((4, rows, lanes), f32), pltpu.VMEM((2, rows, lanes), f32),
                pltpu.VMEM((5, nz, lanes), f32), pltpu.VMEM((3, nz, lanes), f32),
                pltpu.VMEM((5, nz, lanes), f32), pltpu.VMEM((3, nz, lanes), f32),
                pltpu.VMEM((2, 2, 1, lanes), f32), pltpu.VMEM((4, 2, 1, lanes), f32),
                pltpu.VMEM((rows, lanes), f32), pltpu.VMEM((rows, lanes), f32),
                pltpu.VMEM((2, nz, lanes), f32), pltpu.VMEM((2, nz, lanes), f32), pltpu.VMEM((2, nz, lanes), f32),
                pltpu.VMEM((1, 1, lanes), f32), pltpu.VMEM((nlat, 1, lanes), f32),
                pltpu.VMEM((nlon, 1, lanes), f32), pltpu.VMEM((1, 1, lanes), f32),
                pltpu.SemaphoreType.DMA((6,)), pltpu.SemaphoreType.DMA((10,)), pltpu.SemaphoreType.DMA((10,)),
                pltpu.SemaphoreType.DMA((3,)), pltpu.SemaphoreType.DMA((3,)),
            ],
            compiler_params=pltpu.CompilerParams(collective_id=0, has_side_effects=True, vmem_limit_bytes=32 * 1024 * 1024),
        )(*[pltpu.with_memory_space_constraint(one, pltpu.HBM) for one in flat])
        w, z = w.reshape(rhs.shape), z.reshape(rhs.shape)
        c = [one[:, None, None, :] for one in coef]
        return c[0] * rhs + c[1] * w, c[2] * rhs + c[3] * w + c[4] * z

    return jax.shard_map(
        body,
        mesh=mesh,
        in_specs=(
            P(None, None, "lat", "lon"),
            P(None, "lat", "lon"),
            P("lat", "lon"),
            P(None, "lat", "lon"),
            P(None, "lat", "lon"),
            P(None, "lat", "lon"),
        ),
        out_specs=(P(None, None, "lat", "lon"), P(None, None, "lat", "lon")),
        check_vma=False,
    )
```

```python
import jax
import jax.numpy as jnp
from jax import lax
from jax.experimental import pallas as pl
from jax.experimental.pallas import tpu as pltpu
from jax.sharding import PartitionSpec as P

MESH = pl.DeviceIdType.MESH
UNROLL = 16
HUB = 1


def kernel(nlon, nlat, rhs, mask_in, levels_in, ed_in, nd_in, vd_in,
           w_out, z_out, coef0, coef1, coef2, coef3, coef4,
           bp, maskv, levelsv, edv, ndv, vdv,
           ocp, edp, ndp, ce, cw, cn, cs, cd,
           col_out, from_east, from_west,
           row0_out, row15_out, from_north, from_south,
           corner_out, corner_in, wcol_out, wcol_west, wrow_out, wrow_south, zrow_north,
           part, hub_in, peer_in, total,
           in_sem, send_sem, recv_sem, hub_send, hub_recv):
    rows, lanes = levels_in.shape
    nz = mask_in.shape[0] // rows
    lon, lat = lax.axis_index("lon"), lax.axis_index("lat")
    lon_east, lon_west = lax.rem(lon + 1, nlon), lax.rem(lon + nlon - 1, nlon)
    lat_north, lat_south = lax.rem(lat + 1, nlat), lax.rem(lat + nlat - 1, nlat)
    east, west = {"lon": lon_east}, {"lon": lon_west}
    north, south = {"lat": lat_north}, {"lat": lat_south}
    north_east = {"lon": lon_east, "lat": lat_north}
    north_west = {"lon": lon_west, "lat": lat_north}
    south_east = {"lon": lon_east, "lat": lat_south}
    south_west = {"lon": lon_west, "lat": lat_south}
    is_hub = lat == HUB

    barrier = pltpu.get_barrier_semaphore()
    for target in (east, west, north, south, north_east, north_west, south_east):
        pl.semaphore_signal(barrier, 1, device_id=target, device_id_type=MESH)

    loads = [
        pltpu.make_async_copy(mask_in, maskv, in_sem.at[0]),
        pltpu.make_async_copy(levels_in, levelsv, in_sem.at[1]),
        pltpu.make_async_copy(ed_in, edv, in_sem.at[2]),
        pltpu.make_async_copy(nd_in, ndv, in_sem.at[3]),
        pltpu.make_async_copy(vd_in, vdv, in_sem.at[4]),
        pltpu.make_async_copy(rhs, bp, in_sem.at[5]),
    ]
    for load in loads:
        load.start()

    @pl.when(is_hub)
    def _():
        def tell_member(d, carry):
            pl.semaphore_signal(barrier, 1, device_id={"lat": lax.rem(lat + d, nlat)}, device_id_type=MESH)
            return carry

        lax.fori_loop(1, nlat, tell_member, 0)

        def tell_peer(d, carry):
            pl.semaphore_signal(barrier, 1, device_id={"lon": lax.rem(lon + d, nlon)}, device_id_type=MESH)
            return carry

        lax.fori_loop(1, nlon, tell_peer, 0)

    lane2 = lax.broadcasted_iota(jnp.int32, (rows, lanes), 1)
    row2 = lax.broadcasted_iota(jnp.int32, (rows, lanes), 0)
    lane1 = lax.broadcasted_iota(jnp.int32, (1, lanes), 1)
    lane_z = lax.broadcasted_iota(jnp.int32, (nz, lanes), 1)
    row_z = lax.broadcasted_iota(jnp.int32, (nz, lanes), 0)
    first_row, last_row = row2 == 0, row2 == rows - 1
    first_lane, last_lane = lane2 == 0, lane2 == lanes - 1
    edge_lane = first_lane | last_lane
    pair = lane2 // 2
    even, even1 = lane2 % 2 == 0, lane1 % 2 == 0
    zero = jnp.zeros((rows, lanes), jnp.float32)

    def at(k):
        return pl.ds(pl.multiple_of(k * rows, rows), rows)

    def over_levels(step, carry=0):
        def several(n, carry):
            for i in range(UNROLL):
                carry = step(n * UNROLL + i, carry)
            return carry

        return lax.fori_loop(0, nz // UNROLL, several, carry)

    row0, row15 = pl.ds(0, nz, stride=rows), pl.ds(rows - 1, nz, stride=rows)

    def turn(piece, shift, axis=1):
        if isinstance(shift, int):
            shift = shift % piece.shape[axis]
        return pltpu.roll(piece, shift, axis)

    def pack(piece, j, into):
        return jnp.where(pair == j, turn(piece, 2 * j + 1), into)

    def unpack(packed, j):
        return jnp.where(edge_lane, turn(packed, lanes - 1 - 2 * j), 0.0)

    def facing(east_packed, west_packed):
        return jnp.where(even if east_packed.shape[0] == rows else even1, turn(east_packed, -1), turn(west_packed, 1))

    def both(packed):
        return packed + turn(packed, 2 * nz)

    def inside(field, t, k):
        v = field[t, at(k)]
        flows = (ce[at(k)] * (v - turn(v, -1)) + cw[at(k)] * (v - turn(v, 1))) + (
            cn[at(k)] * (v - turn(v, -1, 0)) + cs[at(k)] * (v - turn(v, 1, 0)))
        below, above = field[t, at(jnp.minimum(k + 1, nz - 1))], field[t, at(jnp.maximum(k - 1, 0))]
        return v, flows + (cd[at(k + 1)] * (v - below) + cd[at(k)] * (v - above))

    loads[0].wait()
    loads[1].wait()
    @over_levels
    def _(k, carry):
        ocp[at(k)] = jnp.where((maskv[at(k)] == 1) & (levelsv[...] > k), 1.0, 0.0)
        return carry

    ocp[at(nz)] = zero
    cd[at(0)] = zero
    for load in loads[2:5]:
        load.wait()

    @over_levels
    def _(k, carry):
        oc = ocp[at(k)]
        edp[at(k)] = edv[at(k)].astype(jnp.float32) * oc
        ndp[at(k)] = ndv[at(k)].astype(jnp.float32) * oc
        cd[at(k + 1)] = vdv[at(k)].astype(jnp.float32) * oc * ocp[at(k + 1)]
        return carry

    def faces(k, carry):
        edge_coef, edge_nd = carry
        oc, ed, nd = ocp[at(k)], edp[at(k)], ndp[at(k)]
        ce[at(k)] = jnp.where(last_lane, 0.0, ed * turn(oc, -1))
        cw[at(k)] = jnp.where(first_lane, 0.0, turn(ed, 1) * oc)
        cn[at(k)] = jnp.where(last_row, 0.0, nd * turn(oc, -1, 0))
        cs[at(k)] = jnp.where(first_row, 0.0, turn(nd, 1, 0) * oc)
        return pack(jnp.where(last_lane, ed, oc), k, edge_coef), pack(nd, k, edge_nd)

    edge_coef, edge_nd = over_levels(faces, (zero, zero))
    edge_coef, edge_nd = both(edge_coef), both(edge_nd)
    row0_out[2] = ocp[row0]
    row15_out[2] = ndp[row15]
    loads[5].wait()

    def inner(k, carry):
        edge_b, edge_p, *squares = carry
        for t in range(2):
            v, flows = inside(bp, t, k)
            w_out[t, at(k)] = flows
            squares[t] = squares[t] + v * v
            j = t * nz + k
            edge_b, edge_p = pack(v, j, edge_b), pack(flows, j, edge_p)
        return edge_b, edge_p, *squares

    edge_b, edge_p, *squares = over_levels(inner, (zero,) * 4)
    sums = [[one] for one in squares]
    for t in range(2):
        row0_out[t] = bp[t, row0]
        row15_out[t] = bp[t, row15]
        row0_out[3 + t] = w_out[t, row0]
    col_out[0], col_out[1], col_out[2], col_out[3] = edge_b, edge_coef, edge_p, edge_nd
    corner_out[0, 0], corner_out[0, 1] = edge_b[0:1], edge_coef[0:1]
    corner_out[1, 0], corner_out[1, 1] = edge_b[rows - 1:rows], edge_nd[rows - 1:rows]

    pl.semaphore_wait(barrier, jnp.where(is_hub, nlon + 6, 8))

    def send(source, target, number, device):
        copy = pltpu.make_async_remote_copy(
            source, target, send_sem.at[number], recv_sem.at[number], device_id=device, device_id_type=MESH)
        copy.start()
        return copy

    halo = [
        send(col_out, from_east, 0, west),
        send(col_out.at[pl.ds(0, 2)], from_west, 1, east),
        send(corner_out.at[0], corner_in.at[1], 2, south_west),
        send(corner_out.at[0], corner_in.at[2], 3, south_east),
        send(corner_out.at[1], corner_in.at[3], 4, north_west),
        send(corner_out.at[0], corner_in.at[0], 5, south),
        send(row0_out, from_north, 6, south),
        send(row15_out, from_south, 7, north),
    ]
    for copy in halo:
        copy.wait_recv()

    top = jnp.where(lat == nlat - 1, 0.0, 1.0)
    bottom = jnp.where(lat == 0, 0.0, 1.0)
    cross = edge_coef * facing(from_east[1], from_west[1])
    faced_b = facing(from_east[0], from_west[0])
    flow = cross * (edge_b - faced_b)
    ghost = turn(from_east[2], -1) - flow
    ne_b, ne_oc = turn(corner_in[1, 0], -1), turn(corner_in[1, 1], -1)
    se_b, se_nd = turn(corner_in[3, 0], -1), turn(corner_in[3, 1], -1)
    east_oc, east_nd = turn(from_east[1], -1), turn(from_east[3], -1)
    ghost = ghost + jnp.where(last_row, (east_nd * (ne_oc * top)) * (faced_b - ne_b), 0.0)
    ghost = ghost + jnp.where(first_row, (east_oc * (se_nd * bottom)) * (faced_b - se_b), 0.0)
    flow_ghost = (corner_in[0, 1] * facing(corner_in[1, 1], corner_in[2, 1])) * (
        corner_in[0, 0] - facing(corner_in[1, 0], corner_in[2, 0]))
    c_north = row15_out[2] * (from_north[2] * top)
    c_south = (from_south[2] * bottom) * row0_out[2]
    north_ghost = []
    for t in range(2):
        out_north = c_north * (row15_out[t] - from_north[t])
        w_out[t, row15] = w_out[t, row15] + out_north
        w_out[t, row0] = w_out[t, row0] + c_south * (row0_out[t] - from_south[t])
        place = 2 * (t * nz + row_z)
        spread_ghost = jnp.broadcast_to(flow_ghost, (nz, lanes))
        east_end = jnp.sum(jnp.where(lane_z == place, spread_ghost, 0.0), axis=1, keepdims=True)
        west_end = jnp.sum(jnp.where(lane_z == place + 1, spread_ghost, 0.0), axis=1, keepdims=True)
        ends = jnp.where(lane_z == lanes - 1, east_end, jnp.where(lane_z == 0, west_end, 0.0))
        north_ghost.append(from_north[3 + t] - out_north + ends)

    def complete(k, carry):
        edge_w, *dots = carry
        for t in range(2):
            v = bp[t, at(k)]
            j = t * nz + k
            w = w_out[t, at(k)] + unpack(flow, j)
            w_out[t, at(k)] = w
            dots[2 * t], dots[2 * t + 1] = dots[2 * t] + v * w, dots[2 * t + 1] + w * w
            edge_w = pack(w, j, edge_w)
        return edge_w, *dots

    edge_w, *dots = over_levels(complete, (zero,) * 5)
    for t in range(2):
        sums[t] += dots[2 * t:2 * t + 2]
        wrow_out[t] = w_out[t, row15]
    wcol_out[...] = edge_w
    later = [
        send(wcol_out, wcol_west, 8, east),
        send(wrow_out, wrow_south, 9, north),
    ]
    gap = edge_w - ghost
    east_sum = jnp.where(even, (cross * gap) * gap, 0.0)

    def energy(k, carry):
        carry = list(carry)
        for t in range(2):
            w = w_out[t, at(k)]
            gap_east, gap_north = w - turn(w, -1), w - turn(w, -1, 0)
            gap_down = w - w_out[t, at(jnp.minimum(k + 1, nz - 1))]
            carry[t] = carry[t] + (((ce[at(k)] * gap_east) * gap_east + (cn[at(k)] * gap_north) * gap_north)
                                   + (cd[at(k + 1)] * gap_down) * gap_down)
        return tuple(carry)

    cubes = over_levels(energy, tuple(jnp.where(lane2 // (2 * nz) == t, east_sum, 0.0) for t in range(2)))
    for t in range(2):
        s3 = cubes[t]
        gap = wrow_out[t] - north_ghost[t]
        out_north = c_north * gap
        zrow_north[t] = out_north
        row_sum = out_north * gap
        for k in range(nz // rows):
            s3 = s3 + row_sum[k * rows:(k + 1) * rows]
        sums[t].append(s3)

    mine = jnp.zeros((rows // 2, lanes), jnp.float32)
    for t in range(2):
        for j in range(4):
            one = jnp.sum(sums[t][j][:rows // 2] + sums[t][j][rows // 2:], axis=1, keepdims=True)
            mine = jnp.where(lane2[:rows // 2] == t * 4 + j, one, mine)
    mine = jnp.sum(mine, axis=0, keepdims=True)
    part[0] = mine

    @pl.when(jnp.logical_not(is_hub))
    def _():
        slot = lax.rem(lat - HUB + nlat, nlat)
        give = pltpu.make_async_remote_copy(
            part.at[0], hub_in.at[slot], hub_send.at[0], hub_recv.at[0],
            device_id={"lat": HUB}, device_id_type=MESH)
        give.start()
        give.wait_send()
    for copy in later:
        copy.wait_recv()
    flow = cross * (edge_w - jnp.where(even, ghost, turn(wcol_west[...], 1)))

    @over_levels
    def _(k, carry):
        for t in range(2):
            z_out[t, at(k)] = inside(w_out, t, k)[1] + unpack(flow, t * nz + k)
        return carry

    for t in range(2):
        z_out[t, row15] = z_out[t, row15] + zrow_north[t]
        z_out[t, row0] = z_out[t, row0] + c_south * (w_out[t, row0] - wrow_south[t])

    @pl.when(jnp.logical_not(is_hub))
    def _():
        pltpu.make_async_copy(total.at[0], total.at[0], hub_recv.at[2]).wait()

    @pl.when(is_hub)
    def _():
        members = hub_in.at[pl.ds(1, nlat - 1)]
        peers = peer_in.at[pl.ds(1, nlon - 1)]
        hub_in[0] = part[0]
        pltpu.make_async_copy(members, members, hub_recv.at[0]).wait()
        peer_in[0] = jnp.sum(hub_in[...], axis=0)

        def give_peer(d, carry):
            pltpu.make_async_remote_copy(
                peer_in.at[0], peer_in.at[d], hub_send.at[1], hub_recv.at[1],
                device_id={"lon": lax.rem(lon + d, nlon)}, device_id_type=MESH).start()
            return carry

        lax.fori_loop(1, nlon, give_peer, 0)
        pltpu.make_async_copy(peers, peers, hub_recv.at[1]).wait()
        total[0] = jnp.sum(peer_in[...], axis=0)

        def give_member(d, carry):
            pltpu.make_async_remote_copy(
                total.at[0], total.at[0], hub_send.at[2], hub_recv.at[2],
                device_id={"lat": lax.rem(lat + d, nlat)}, device_id_type=MESH).start()
            return carry

        lax.fori_loop(1, nlat, give_member, 0)

    got = total[0]
    for t in range(2):
        m0, l1, l2, l3 = [jnp.sum(jnp.where(lane1 == t * 4 + j, got, 0.0), axis=1, keepdims=True) for j in range(4)]
        c0 = l1 / m0
        a0 = m0 / (m0 + l1)
        spread = l2 - l1 * c0
        curve = l3 - c0 * (2.0 * l2 - c0 * l1)
        beta = a0 * a0 * spread / m0
        a1 = spread / (spread + curve - a0 * spread * (spread / m0))
        g = a0 * c0 + beta
        values = (a0 + a1 * g, -a1 * a0, a0 * c0 - a1 * g, a1 * a0 - a0 - a1 * g, a1 * a0)
        for coef, value in zip((coef0, coef1, coef2, coef3, coef4), values, strict=True):
            coef[t:t + 1] = jnp.broadcast_to(value, (1, lanes))

    for copy in halo + later:
        copy.wait_send()

    @pl.when(is_hub)
    def _():
        peers, members = peer_in.at[pl.ds(1, nlon - 1)], hub_in.at[pl.ds(1, nlat - 1)]
        pltpu.make_async_copy(peers, peers, hub_send.at[1]).wait()
        pltpu.make_async_copy(members, members, hub_send.at[2]).wait()


def solution(mesh):
    nlon, nlat = mesh.shape["lon"], mesh.shape["lat"]

    def body(rhs, sea_mask, levels, ed, nd, vd):
        tracers, nz, rows, lanes = rhs.shape
        field, block = (tracers, nz * rows, lanes), (nz * rows, lanes)
        taller = ((nz + 1) * rows, lanes)
        flat = [rhs.reshape(field), sea_mask.reshape(block), levels] + [one.reshape(block) for one in (ed, nd, vd)]
        f32 = jnp.float32
        whole = pl.BlockSpec(memory_space=pltpu.VMEM)
        w, z, *coef = pl.pallas_call(
            lambda *refs: kernel(nlon, nlat, *refs),
            out_shape=(
                jax.ShapeDtypeStruct(field, f32),
                jax.ShapeDtypeStruct(field, f32),
            ) + (jax.ShapeDtypeStruct((tracers, lanes), f32),) * 5,
            in_specs=[pl.BlockSpec(memory_space=pltpu.HBM)] * 6,
            out_specs=(whole,) * 7,
            scratch_shapes=[
                pltpu.VMEM(field, f32),
                pltpu.VMEM(block, jnp.int32), pltpu.VMEM((rows, lanes), jnp.int32),
                pltpu.VMEM(block, jnp.bfloat16), pltpu.VMEM(block, jnp.bfloat16), pltpu.VMEM(block, jnp.bfloat16),
                pltpu.VMEM(taller, f32), pltpu.VMEM(block, f32), pltpu.VMEM(block, f32),
                pltpu.VMEM(block, f32), pltpu.VMEM(block, f32), pltpu.VMEM(block, f32), pltpu.VMEM(block, f32),
                pltpu.VMEM(taller, f32),
                pltpu.VMEM((4, rows, lanes), f32), pltpu.VMEM((4, rows, lanes), f32), pltpu.VMEM((2, rows, lanes), f32),
                pltpu.VMEM((5, nz, lanes), f32), pltpu.VMEM((3, nz, lanes), f32),
                pltpu.VMEM((5, nz, lanes), f32), pltpu.VMEM((3, nz, lanes), f32),
                pltpu.VMEM((2, 2, 1, lanes), f32), pltpu.VMEM((4, 2, 1, lanes), f32),
                pltpu.VMEM((rows, lanes), f32), pltpu.VMEM((rows, lanes), f32),
                pltpu.VMEM((2, nz, lanes), f32), pltpu.VMEM((2, nz, lanes), f32), pltpu.VMEM((2, nz, lanes), f32),
                pltpu.VMEM((1, 1, lanes), f32), pltpu.VMEM((nlat, 1, lanes), f32),
                pltpu.VMEM((nlon, 1, lanes), f32), pltpu.VMEM((1, 1, lanes), f32),
                pltpu.SemaphoreType.DMA((6,)), pltpu.SemaphoreType.DMA((10,)), pltpu.SemaphoreType.DMA((10,)),
                pltpu.SemaphoreType.DMA((3,)), pltpu.SemaphoreType.DMA((3,)),
            ],
            compiler_params=pltpu.CompilerParams(collective_id=0, has_side_effects=True, vmem_limit_bytes=32 * 1024 * 1024),
        )(*[pltpu.with_memory_space_constraint(one, pltpu.HBM) for one in flat])
        w, z = w.reshape(rhs.shape), z.reshape(rhs.shape)
        c = [one[:, None, None, :] for one in coef]
        return c[0] * rhs + c[1] * w, c[2] * rhs + c[3] * w + c[4] * z

    return jax.shard_map(
        body,
        mesh=mesh,
        in_specs=(
            P(None, None, "lat", "lon"),
            P(None, "lat", "lon"),
            P("lat", "lon"),
            P(None, "lat", "lon"),
            P(None, "lat", "lon"),
            P(None, "lat", "lon"),
        ),
        out_specs=(P(None, None, "lat", "lon"), P(None, None, "lat", "lon")),
        check_vma=False,
    )
```

```python
import jax
import jax.numpy as jnp
from jax import lax
from jax.experimental import pallas as pl
from jax.experimental.pallas import tpu as pltpu
from jax.sharding import PartitionSpec as P

MESH = pl.DeviceIdType.MESH
UNROLL = 16
PARTS = 2
HUB = 1


def kernel(nlon, nlat, rhs, mask_in, levels_in, ed_in, nd_in, vd_in,
           bp, w_out, z_out, coef0, coef1, coef2, coef3, coef4,
           maskv, levelsv, edv, ndv, vdv,
           ocp, edp, ndp, ce, cw, cn, cs, cd,
           col_out, from_east, from_west,
           row0_out, row15_out, from_north, from_south,
           corner_out, corner_in, wcol_out, wcol_west, wrow_out, wrow_south, zrow_north,
           part, hub_in, peer_in, total,
           in_sem, send_sem, recv_sem, hub_send, hub_recv):
    rows, lanes = levels_in.shape
    nz = mask_in.shape[0] // rows
    lon, lat = lax.axis_index("lon"), lax.axis_index("lat")
    lon_east, lon_west = lax.rem(lon + 1, nlon), lax.rem(lon + nlon - 1, nlon)
    lat_north, lat_south = lax.rem(lat + 1, nlat), lax.rem(lat + nlat - 1, nlat)
    east, west = {"lon": lon_east}, {"lon": lon_west}
    north, south = {"lat": lat_north}, {"lat": lat_south}
    north_east = {"lon": lon_east, "lat": lat_north}
    north_west = {"lon": lon_west, "lat": lat_north}
    south_east = {"lon": lon_east, "lat": lat_south}
    south_west = {"lon": lon_west, "lat": lat_south}
    is_hub = lat == HUB

    barrier = pltpu.get_barrier_semaphore()
    for target in (east, west, north, south, north_east, north_west, south_east):
        pl.semaphore_signal(barrier, 1, device_id=target, device_id_type=MESH)

    loads = [
        pltpu.make_async_copy(mask_in, maskv, in_sem.at[0]),
        pltpu.make_async_copy(levels_in, levelsv, in_sem.at[1]),
        pltpu.make_async_copy(ed_in, edv, in_sem.at[2]),
        pltpu.make_async_copy(nd_in, ndv, in_sem.at[3]),
        pltpu.make_async_copy(vd_in, vdv, in_sem.at[4]),
        pltpu.make_async_copy(rhs, bp, in_sem.at[5]),
    ]
    for load in loads:
        load.start()

    @pl.when(is_hub)
    def _():
        def tell_member(d, carry):
            pl.semaphore_signal(barrier, 1, device_id={"lat": lax.rem(lat + d, nlat)}, device_id_type=MESH)
            return carry

        lax.fori_loop(1, nlat, tell_member, 0)

        def tell_peer(d, carry):
            pl.semaphore_signal(barrier, 1, device_id={"lon": lax.rem(lon + d, nlon)}, device_id_type=MESH)
            return carry

        lax.fori_loop(1, nlon, tell_peer, 0)

    lane2 = lax.broadcasted_iota(jnp.int32, (rows, lanes), 1)
    row2 = lax.broadcasted_iota(jnp.int32, (rows, lanes), 0)
    lane1 = lax.broadcasted_iota(jnp.int32, (1, lanes), 1)
    lane_z = lax.broadcasted_iota(jnp.int32, (nz, lanes), 1)
    row_z = lax.broadcasted_iota(jnp.int32, (nz, lanes), 0)
    first_row, last_row = row2 == 0, row2 == rows - 1
    first_lane, last_lane = lane2 == 0, lane2 == lanes - 1
    edge_lane = first_lane | last_lane
    pair = lane2 // 2
    even, even1 = lane2 % 2 == 0, lane1 % 2 == 0
    zero = jnp.zeros((rows, lanes), jnp.float32)

    def at(k):
        return pl.ds(pl.multiple_of(k * rows, rows), rows)

    def over_levels(step, carry=0):
        def several(n, carry):
            for i in range(UNROLL):
                carry = step(n * UNROLL + i, carry)
            return carry

        return lax.fori_loop(0, nz // UNROLL, several, carry)

    row0, row15 = pl.ds(0, nz, stride=rows), pl.ds(rows - 1, nz, stride=rows)

    def turn(piece, shift, axis=1):
        if isinstance(shift, int):
            shift = shift % piece.shape[axis]
        return pltpu.roll(piece, shift, axis)

    def pack(piece, j, into):
        return jnp.where(pair == j, turn(piece, 2 * j + 1), into)

    def unpack(packed, j):
        return jnp.where(edge_lane, turn(packed, lanes - 1 - 2 * j), 0.0)

    def facing(east_packed, west_packed):
        return jnp.where(even if east_packed.shape[0] == rows else even1, turn(east_packed, -1), turn(west_packed, 1))

    def both(packed):
        return packed + turn(packed, 2 * nz)

    def inside(field, t, k):
        v = field[t, at(k)]
        flows = (ce[at(k)] * (v - turn(v, -1)) + cw[at(k)] * (v - turn(v, 1))) + (
            cn[at(k)] * (v - turn(v, -1, 0)) + cs[at(k)] * (v - turn(v, 1, 0)))
        below, above = field[t, at(jnp.minimum(k + 1, nz - 1))], field[t, at(jnp.maximum(k - 1, 0))]
        return v, flows + (cd[at(k + 1)] * (v - below) + cd[at(k)] * (v - above))

    loads[0].wait()
    loads[1].wait()
    @over_levels
    def _(k, carry):
        ocp[at(k)] = jnp.where((maskv[at(k)] == 1) & (levelsv[...] > k), 1.0, 0.0)
        return carry

    ocp[at(nz)] = zero
    cd[at(0)] = zero
    for load in loads[2:5]:
        load.wait()

    @over_levels
    def _(k, carry):
        oc = ocp[at(k)]
        edp[at(k)] = edv[at(k)].astype(jnp.float32) * oc
        ndp[at(k)] = ndv[at(k)].astype(jnp.float32) * oc
        cd[at(k + 1)] = vdv[at(k)].astype(jnp.float32) * oc * ocp[at(k + 1)]
        return carry

    def faces(k, carry):
        edge_coef, edge_nd = carry
        oc, ed, nd = ocp[at(k)], edp[at(k)], ndp[at(k)]
        ce[at(k)] = jnp.where(last_lane, 0.0, ed * turn(oc, -1))
        cw[at(k)] = jnp.where(first_lane, 0.0, turn(ed, 1) * oc)
        cn[at(k)] = jnp.where(last_row, 0.0, nd * turn(oc, -1, 0))
        cs[at(k)] = jnp.where(first_row, 0.0, turn(nd, 1, 0) * oc)
        return pack(jnp.where(last_lane, ed, oc), k, edge_coef), pack(nd, k, edge_nd)

    edge_coef, edge_nd = over_levels(faces, (zero, zero))
    edge_coef, edge_nd = both(edge_coef), both(edge_nd)
    row0_out[2] = ocp[row0]
    row15_out[2] = ndp[row15]
    loads[5].wait()

    def inner(k, carry):
        edge_b, edge_p, *squares = carry
        for t in range(2):
            v, flows = inside(bp, t, k)
            w_out[t, at(k)] = flows
            squares[t] = squares[t] + v * v
            j = t * nz + k
            edge_b, edge_p = pack(v, j, edge_b), pack(flows, j, edge_p)
        return edge_b, edge_p, *squares

    edge_b, edge_p, *squares = over_levels(inner, (zero,) * 4)
    sums = [[one] for one in squares]
    for t in range(2):
        row0_out[t] = bp[t, row0]
        row15_out[t] = bp[t, row15]
        row0_out[3 + t] = w_out[t, row0]
    col_out[0], col_out[1], col_out[2], col_out[3] = edge_b, edge_coef, edge_p, edge_nd
    corner_out[0, 0], corner_out[0, 1] = edge_b[0:1], edge_coef[0:1]
    corner_out[1, 0], corner_out[1, 1] = edge_b[rows - 1:rows], edge_nd[rows - 1:rows]

    pl.semaphore_wait(barrier, jnp.where(is_hub, nlon + 6, 8))

    def send(source, target, number, device):
        copy = pltpu.make_async_remote_copy(
            source, target, send_sem.at[number], recv_sem.at[number], device_id=device, device_id_type=MESH)
        copy.start()
        return copy

    halo = [
        send(col_out, from_east, 0, west),
        send(col_out.at[pl.ds(0, 2)], from_west, 1, east),
        send(corner_out.at[0], corner_in.at[1], 2, south_west),
        send(corner_out.at[0], corner_in.at[2], 3, south_east),
        send(corner_out.at[1], corner_in.at[3], 4, north_west),
        send(corner_out.at[0], corner_in.at[0], 5, south),
        send(row0_out, from_north, 6, south),
        send(row15_out, from_south, 7, north),
    ]
    for copy in halo:
        copy.wait_recv()

    top = jnp.where(lat == nlat - 1, 0.0, 1.0)
    bottom = jnp.where(lat == 0, 0.0, 1.0)
    cross = edge_coef * facing(from_east[1], from_west[1])
    faced_b = facing(from_east[0], from_west[0])
    flow = cross * (edge_b - faced_b)
    ghost = turn(from_east[2], -1) - flow
    ne_b, ne_oc = turn(corner_in[1, 0], -1), turn(corner_in[1, 1], -1)
    se_b, se_nd = turn(corner_in[3, 0], -1), turn(corner_in[3, 1], -1)
    east_oc, east_nd = turn(from_east[1], -1), turn(from_east[3], -1)
    ghost = ghost + jnp.where(last_row, (east_nd * (ne_oc * top)) * (faced_b - ne_b), 0.0)
    ghost = ghost + jnp.where(first_row, (east_oc * (se_nd * bottom)) * (faced_b - se_b), 0.0)
    flow_ghost = (corner_in[0, 1] * facing(corner_in[1, 1], corner_in[2, 1])) * (
        corner_in[0, 0] - facing(corner_in[1, 0], corner_in[2, 0]))
    c_north = row15_out[2] * (from_north[2] * top)
    c_south = (from_south[2] * bottom) * row0_out[2]
    north_ghost = []
    for t in range(2):
        out_north = c_north * (row15_out[t] - from_north[t])
        w_out[t, row15] = w_out[t, row15] + out_north
        w_out[t, row0] = w_out[t, row0] + c_south * (row0_out[t] - from_south[t])
        place = 2 * (t * nz + row_z)
        spread_ghost = jnp.broadcast_to(flow_ghost, (nz, lanes))
        east_end = jnp.sum(jnp.where(lane_z == place, spread_ghost, 0.0), axis=1, keepdims=True)
        west_end = jnp.sum(jnp.where(lane_z == place + 1, spread_ghost, 0.0), axis=1, keepdims=True)
        ends = jnp.where(lane_z == lanes - 1, east_end, jnp.where(lane_z == 0, west_end, 0.0))
        north_ghost.append(from_north[3 + t] - out_north + ends)

    def complete(k, carry):
        edge_w, *dots = carry
        for t in range(2):
            v = bp[t, at(k)]
            j = t * nz + k
            w = w_out[t, at(k)] + unpack(flow, j)
            w_out[t, at(k)] = w
            dots[2 * t], dots[2 * t + 1] = dots[2 * t] + v * w, dots[2 * t + 1] + w * w
            edge_w = pack(w, j, edge_w)
        return edge_w, *dots

    edge_w, *dots = over_levels(complete, (zero,) * 5)
    for t in range(2):
        sums[t] += dots[2 * t:2 * t + 2]
        wrow_out[t] = w_out[t, row15]
    wcol_out[...] = edge_w
    later = [
        send(wcol_out, wcol_west, 8, east),
        send(wrow_out, wrow_south, 9, north),
    ]
    gap = edge_w - ghost
    east_sum = jnp.where(even, (cross * gap) * gap, 0.0)

    def energy(k, carry):
        carry = list(carry)
        for t in range(2):
            w = w_out[t, at(k)]
            gap_east, gap_north = w - turn(w, -1), w - turn(w, -1, 0)
            gap_down = w - w_out[t, at(jnp.minimum(k + 1, nz - 1))]
            carry[t] = carry[t] + (((ce[at(k)] * gap_east) * gap_east + (cn[at(k)] * gap_north) * gap_north)
                                   + (cd[at(k + 1)] * gap_down) * gap_down)
        return tuple(carry)

    cubes = over_levels(energy, tuple(jnp.where(lane2 // (2 * nz) == t, east_sum, 0.0) for t in range(2)))
    for t in range(2):
        s3 = cubes[t]
        gap = wrow_out[t] - north_ghost[t]
        out_north = c_north * gap
        zrow_north[t] = out_north
        row_sum = out_north * gap
        for k in range(nz // rows):
            s3 = s3 + row_sum[k * rows:(k + 1) * rows]
        sums[t].append(s3)

    mine = jnp.zeros((rows // 2, lanes), jnp.float32)
    for t in range(2):
        for j in range(4):
            one = jnp.sum(sums[t][j][:rows // 2] + sums[t][j][rows // 2:], axis=1, keepdims=True)
            mine = jnp.where(lane2[:rows // 2] == t * 4 + j, one, mine)
    mine = jnp.sum(mine, axis=0, keepdims=True)
    part[0] = mine

    @pl.when(jnp.logical_not(is_hub))
    def _():
        slot = lax.rem(lat - HUB + nlat, nlat)
        give = pltpu.make_async_remote_copy(
            part.at[0], hub_in.at[slot], hub_send.at[0], hub_recv.at[0],
            device_id={"lat": HUB}, device_id_type=MESH)
        give.start()
        give.wait_send()
    for copy in later:
        copy.wait_recv()
    flow = cross * (edge_w - jnp.where(even, ghost, turn(wcol_west[...], 1)))

    @over_levels
    def _(k, carry):
        for t in range(2):
            z_out[t, at(k)] = inside(w_out, t, k)[1] + unpack(flow, t * nz + k)
        return carry

    for t in range(2):
        z_out[t, row15] = z_out[t, row15] + zrow_north[t]
        z_out[t, row0] = z_out[t, row0] + c_south * (w_out[t, row0] - wrow_south[t])

    @pl.when(jnp.logical_not(is_hub))
    def _():
        pltpu.make_async_copy(total.at[0], total.at[0], hub_recv.at[2]).wait()

    @pl.when(is_hub)
    def _():
        members = hub_in.at[pl.ds(1, nlat - 1)]
        peers = peer_in.at[pl.ds(1, nlon - 1)]
        hub_in[0] = part[0]
        pltpu.make_async_copy(members, members, hub_recv.at[0]).wait()
        peer_in[0] = jnp.sum(hub_in[...], axis=0)

        for d in range(1, nlon):
            pltpu.make_async_remote_copy(
                peer_in.at[0], peer_in.at[d], hub_send.at[1], hub_recv.at[1],
                device_id={"lon": lax.rem(lon + d, nlon)}, device_id_type=MESH).start()
        pltpu.make_async_copy(peers, peers, hub_recv.at[1]).wait()
        total[0] = jnp.sum(peer_in[...], axis=0)

        for d in range(1, nlat):
            pltpu.make_async_remote_copy(
                total.at[0], total.at[0], hub_send.at[2], hub_recv.at[2],
                device_id={"lat": (HUB + d) % nlat}, device_id_type=MESH).start()

    got = total[0]
    for t in range(2):
        m0, l1, l2, l3 = [jnp.sum(jnp.where(lane1 == t * 4 + j, got, 0.0), axis=1, keepdims=True) for j in range(4)]
        c0 = l1 / m0
        a0 = m0 / (m0 + l1)
        spread = l2 - l1 * c0
        curve = l3 - c0 * (2.0 * l2 - c0 * l1)
        beta = a0 * a0 * spread / m0
        a1 = spread / (spread + curve - a0 * spread * (spread / m0))
        g = a0 * c0 + beta
        values = (a0 + a1 * g, -a1 * a0, a0 * c0 - a1 * g, a1 * a0 - a0 - a1 * g, a1 * a0)
        for coef, value in zip((coef0, coef1, coef2, coef3, coef4), values, strict=True):
            coef[t:t + 1] = jnp.broadcast_to(value, (1, lanes))

    for copy in halo + later:
        copy.wait_send()

    @pl.when(is_hub)
    def _():
        peers, members = peer_in.at[pl.ds(1, nlon - 1)], hub_in.at[pl.ds(1, nlat - 1)]
        pltpu.make_async_copy(peers, peers, hub_send.at[1]).wait()
        pltpu.make_async_copy(members, members, hub_send.at[2]).wait()


def finish(b, w, z, coef0, coef1, coef2, coef3, coef4, x_out, r_out, x, r, sem):
    part = b.shape[1] // PARTS
    copies = []
    for t in range(2):
        one = slice(t, t + 1)
        for n in range(PARTS):
            at = (t, pl.ds(n * part, part))
            x[at] = coef0[one] * b[at] + coef1[one] * w[at]
            r[at] = (coef2[one] * b[at] + coef3[one] * w[at]) + coef4[one] * z[at]
            for source, target in ((x, x_out), (r, r_out)):
                copies.append(pltpu.make_async_copy(source.at[at], target.at[at], sem.at[len(copies)]))
                copies[-1].start()
    for copy in copies:
        copy.wait()


def solution(mesh):
    nlon, nlat = mesh.shape["lon"], mesh.shape["lat"]

    def body(rhs, sea_mask, levels, ed, nd, vd):
        tracers, nz, rows, lanes = rhs.shape
        field, block = (tracers, nz * rows, lanes), (nz * rows, lanes)
        taller = ((nz + 1) * rows, lanes)
        flat = [rhs.reshape(field), sea_mask.reshape(block), levels] + [one.reshape(block) for one in (ed, nd, vd)]
        f32 = jnp.float32
        whole = pl.BlockSpec(memory_space=pltpu.VMEM)
        fields = pl.pallas_call(
            lambda *refs: kernel(nlon, nlat, *refs),
            out_shape=(jax.ShapeDtypeStruct(field, f32),) * 3 + (jax.ShapeDtypeStruct((tracers, lanes), f32),) * 5,
            in_specs=[pl.BlockSpec(memory_space=pltpu.HBM)] * 6,
            out_specs=(whole,) * 8,
            scratch_shapes=[
                pltpu.VMEM(block, jnp.int32), pltpu.VMEM((rows, lanes), jnp.int32),
                pltpu.VMEM(block, jnp.bfloat16), pltpu.VMEM(block, jnp.bfloat16), pltpu.VMEM(block, jnp.bfloat16),
                pltpu.VMEM(taller, f32), pltpu.VMEM(block, f32), pltpu.VMEM(block, f32),
                pltpu.VMEM(block, f32), pltpu.VMEM(block, f32), pltpu.VMEM(block, f32), pltpu.VMEM(block, f32),
                pltpu.VMEM(taller, f32),
                pltpu.VMEM((4, rows, lanes), f32), pltpu.VMEM((4, rows, lanes), f32), pltpu.VMEM((2, rows, lanes), f32),
                pltpu.VMEM((5, nz, lanes), f32), pltpu.VMEM((3, nz, lanes), f32),
                pltpu.VMEM((5, nz, lanes), f32), pltpu.VMEM((3, nz, lanes), f32),
                pltpu.VMEM((2, 2, 1, lanes), f32), pltpu.VMEM((4, 2, 1, lanes), f32),
                pltpu.VMEM((rows, lanes), f32), pltpu.VMEM((rows, lanes), f32),
                pltpu.VMEM((2, nz, lanes), f32), pltpu.VMEM((2, nz, lanes), f32), pltpu.VMEM((2, nz, lanes), f32),
                pltpu.VMEM((1, 1, lanes), f32), pltpu.VMEM((nlat, 1, lanes), f32),
                pltpu.VMEM((nlon, 1, lanes), f32), pltpu.VMEM((1, 1, lanes), f32),
                pltpu.SemaphoreType.DMA((6,)), pltpu.SemaphoreType.DMA((10,)), pltpu.SemaphoreType.DMA((10,)),
                pltpu.SemaphoreType.DMA((3,)), pltpu.SemaphoreType.DMA((3,)),
            ],
            compiler_params=pltpu.CompilerParams(collective_id=0, has_side_effects=True, vmem_limit_bytes=32 * 1024 * 1024),
        )(*[pltpu.with_memory_space_constraint(one, pltpu.HBM) for one in flat])
        in_place = pl.BlockSpec(memory_space=pltpu.HBM)
        solved = pl.pallas_call(
            finish,
            out_shape=(jax.ShapeDtypeStruct(field, f32),) * 2,
            in_specs=[whole] * 8,
            out_specs=(in_place,) * 2,
            scratch_shapes=[pltpu.VMEM(field, f32), pltpu.VMEM(field, f32), pltpu.SemaphoreType.DMA((4 * PARTS,))],
            compiler_params=pltpu.CompilerParams(vmem_limit_bytes=16 * 1024 * 1024),
        )(*fields)
        return tuple(one.reshape(rhs.shape) for one in solved)

    return jax.shard_map(
        body,
        mesh=mesh,
        in_specs=(
            P(None, None, "lat", "lon"),
            P(None, "lat", "lon"),
            P("lat", "lon"),
            P(None, "lat", "lon"),
            P(None, "lat", "lon"),
            P(None, "lat", "lon"),
        ),
        out_specs=(P(None, None, "lat", "lon"), P(None, None, "lat", "lon")),
        check_vma=False,
    )
```

```python
import jax
import jax.numpy as jnp
from jax import lax
from jax.experimental import pallas as pl
from jax.experimental.pallas import tpu as pltpu
from jax.sharding import PartitionSpec as P

MESH = pl.DeviceIdType.MESH
UNROLL = 16
PARTS = 2
HUB = 1


def kernel(nlon, nlat, rhs, mask_in, levels_in, ed_in, nd_in, vd_in,
           bp, w_out, z_out, coef0, coef1, coef2, coef3, coef4,
           maskv, levelsv, edv, ndv, vdv,
           ocp, edp, ndp, ce, cw, cn, cs, cd,
           col_out, from_east, from_west,
           row0_out, row15_out, from_north, from_south,
           corner_out, corner_in, wcol_out, wcol_west, wrow_out, wrow_south, zrow_north,
           part, hub_in, peer_in, total,
           in_sem, send_sem, recv_sem, hub_send, hub_recv):
    rows, lanes = levels_in.shape
    nz = mask_in.shape[0] // rows
    lon, lat = lax.axis_index("lon"), lax.axis_index("lat")
    lon_east, lon_west = lax.rem(lon + 1, nlon), lax.rem(lon + nlon - 1, nlon)
    lat_north, lat_south = lax.rem(lat + 1, nlat), lax.rem(lat + nlat - 1, nlat)
    east, west = {"lon": lon_east}, {"lon": lon_west}
    north, south = {"lat": lat_north}, {"lat": lat_south}
    north_east = {"lon": lon_east, "lat": lat_north}
    north_west = {"lon": lon_west, "lat": lat_north}
    south_east = {"lon": lon_east, "lat": lat_south}
    south_west = {"lon": lon_west, "lat": lat_south}
    is_hub = lat == HUB

    barrier = pltpu.get_barrier_semaphore()
    for target in (east, west, north, south, north_east, north_west, south_east):
        pl.semaphore_signal(barrier, 1, device_id=target, device_id_type=MESH)

    loads = [
        pltpu.make_async_copy(mask_in, maskv, in_sem.at[0]),
        pltpu.make_async_copy(levels_in, levelsv, in_sem.at[1]),
        pltpu.make_async_copy(ed_in, edv, in_sem.at[2]),
        pltpu.make_async_copy(nd_in, ndv, in_sem.at[3]),
        pltpu.make_async_copy(vd_in, vdv, in_sem.at[4]),
        pltpu.make_async_copy(rhs, bp, in_sem.at[5]),
    ]
    for load in loads:
        load.start()

    @pl.when(is_hub)
    def _():
        def tell_member(d, carry):
            pl.semaphore_signal(barrier, 1, device_id={"lat": lax.rem(lat + d, nlat)}, device_id_type=MESH)
            return carry

        lax.fori_loop(1, nlat, tell_member, 0)

        def tell_peer(d, carry):
            pl.semaphore_signal(barrier, 1, device_id={"lon": lax.rem(lon + d, nlon)}, device_id_type=MESH)
            return carry

        lax.fori_loop(1, nlon, tell_peer, 0)

    lane2 = lax.broadcasted_iota(jnp.int32, (rows, lanes), 1)
    row2 = lax.broadcasted_iota(jnp.int32, (rows, lanes), 0)
    lane1 = lax.broadcasted_iota(jnp.int32, (1, lanes), 1)
    lane_z = lax.broadcasted_iota(jnp.int32, (nz, lanes), 1)
    row_z = lax.broadcasted_iota(jnp.int32, (nz, lanes), 0)
    first_row, last_row = row2 == 0, row2 == rows - 1
    first_lane, last_lane = lane2 == 0, lane2 == lanes - 1
    edge_lane = first_lane | last_lane
    pair = lane2 // 2
    even, even1 = lane2 % 2 == 0, lane1 % 2 == 0
    zero = jnp.zeros((rows, lanes), jnp.float32)

    def at(k):
        return pl.ds(pl.multiple_of(k * rows, rows), rows)

    def over_levels(step, carry=0):
        def several(n, carry):
            for i in range(UNROLL):
                carry = step(n * UNROLL + i, carry)
            return carry

        return lax.fori_loop(0, nz // UNROLL, several, carry)

    row0, row15 = pl.ds(0, nz, stride=rows), pl.ds(rows - 1, nz, stride=rows)

    def turn(piece, shift, axis=1):
        if isinstance(shift, int):
            shift = shift % piece.shape[axis]
        return pltpu.roll(piece, shift, axis)

    def pack(piece, j, into):
        return jnp.where(pair == j, turn(piece, 2 * j + 1), into)

    def unpack(packed, j):
        return jnp.where(edge_lane, turn(packed, lanes - 1 - 2 * j), 0.0)

    def facing(east_packed, west_packed):
        return jnp.where(even if east_packed.shape[0] == rows else even1, turn(east_packed, -1), turn(west_packed, 1))

    def both(packed):
        return packed + turn(packed, 2 * nz)

    def inside(field, t, k):
        v = field[t, at(k)]
        flows = (ce[at(k)] * (v - turn(v, -1)) + cw[at(k)] * (v - turn(v, 1))) + (
            cn[at(k)] * (v - turn(v, -1, 0)) + cs[at(k)] * (v - turn(v, 1, 0)))
        below, above = field[t, at(jnp.minimum(k + 1, nz - 1))], field[t, at(jnp.maximum(k - 1, 0))]
        return v, flows + (cd[at(k + 1)] * (v - below) + cd[at(k)] * (v - above))

    loads[0].wait()
    loads[1].wait()
    @over_levels
    def _(k, carry):
        ocp[at(k)] = jnp.where((maskv[at(k)] == 1) & (levelsv[...] > k), 1.0, 0.0)
        return carry

    ocp[at(nz)] = zero
    cd[at(0)] = zero
    for load in loads[2:5]:
        load.wait()

    @over_levels
    def _(k, carry):
        oc = ocp[at(k)]
        edp[at(k)] = edv[at(k)].astype(jnp.float32) * oc
        ndp[at(k)] = ndv[at(k)].astype(jnp.float32) * oc
        cd[at(k + 1)] = vdv[at(k)].astype(jnp.float32) * oc * ocp[at(k + 1)]
        return carry

    def faces(k, carry):
        edge_coef, edge_nd = carry
        oc, ed, nd = ocp[at(k)], edp[at(k)], ndp[at(k)]
        ce[at(k)] = jnp.where(last_lane, 0.0, ed * turn(oc, -1))
        cw[at(k)] = jnp.where(first_lane, 0.0, turn(ed, 1) * oc)
        cn[at(k)] = jnp.where(last_row, 0.0, nd * turn(oc, -1, 0))
        cs[at(k)] = jnp.where(first_row, 0.0, turn(nd, 1, 0) * oc)
        return pack(jnp.where(last_lane, ed, oc), k, edge_coef), pack(nd, k, edge_nd)

    edge_coef, edge_nd = over_levels(faces, (zero, zero))
    edge_coef, edge_nd = both(edge_coef), both(edge_nd)
    row0_out[2] = ocp[row0]
    row15_out[2] = ndp[row15]
    loads[5].wait()

    def inner(k, carry):
        edge_b, edge_p, *squares = carry
        for t in range(2):
            v, flows = inside(bp, t, k)
            w_out[t, at(k)] = flows
            squares[t] = squares[t] + v * v
            j = t * nz + k
            edge_b, edge_p = pack(v, j, edge_b), pack(flows, j, edge_p)
        return edge_b, edge_p, *squares

    edge_b, edge_p, *squares = over_levels(inner, (zero,) * 4)
    sums = [[one] for one in squares]
    for t in range(2):
        row0_out[t] = bp[t, row0]
        row15_out[t] = bp[t, row15]
        row0_out[3 + t] = w_out[t, row0]
    col_out[0], col_out[1], col_out[2], col_out[3] = edge_b, edge_coef, edge_p, edge_nd
    corner_out[0, 0], corner_out[0, 1] = edge_b[0:1], edge_coef[0:1]
    corner_out[1, 0], corner_out[1, 1] = edge_b[rows - 1:rows], edge_nd[rows - 1:rows]

    pl.semaphore_wait(barrier, jnp.where(is_hub, nlon + 6, 8))

    def send(source, target, number, device):
        copy = pltpu.make_async_remote_copy(
            source, target, send_sem.at[number], recv_sem.at[number], device_id=device, device_id_type=MESH)
        copy.start()
        return copy

    halo = [
        send(corner_out.at[0], corner_in.at[1], 2, south_west),
        send(corner_out.at[0], corner_in.at[2], 3, south_east),
        send(corner_out.at[1], corner_in.at[3], 4, north_west),
        send(corner_out.at[0], corner_in.at[0], 5, south),
        send(row0_out, from_north, 6, south),
        send(row15_out, from_south, 7, north),
        send(col_out, from_east, 0, west),
        send(col_out.at[pl.ds(0, 2)], from_west, 1, east),
    ]
    for copy in halo:
        copy.wait_recv()

    top = jnp.where(lat == nlat - 1, 0.0, 1.0)
    bottom = jnp.where(lat == 0, 0.0, 1.0)
    cross = edge_coef * facing(from_east[1], from_west[1])
    faced_b = facing(from_east[0], from_west[0])
    flow = cross * (edge_b - faced_b)
    ghost = turn(from_east[2], -1) - flow
    ne_b, ne_oc = turn(corner_in[1, 0], -1), turn(corner_in[1, 1], -1)
    se_b, se_nd = turn(corner_in[3, 0], -1), turn(corner_in[3, 1], -1)
    east_oc, east_nd = turn(from_east[1], -1), turn(from_east[3], -1)
    ghost = ghost + jnp.where(last_row, (east_nd * (ne_oc * top)) * (faced_b - ne_b), 0.0)
    ghost = ghost + jnp.where(first_row, (east_oc * (se_nd * bottom)) * (faced_b - se_b), 0.0)
    flow_ghost = (corner_in[0, 1] * facing(corner_in[1, 1], corner_in[2, 1])) * (
        corner_in[0, 0] - facing(corner_in[1, 0], corner_in[2, 0]))
    c_north = row15_out[2] * (from_north[2] * top)
    c_south = (from_south[2] * bottom) * row0_out[2]
    north_ghost = []
    for t in range(2):
        out_north = c_north * (row15_out[t] - from_north[t])
        w_out[t, row15] = w_out[t, row15] + out_north
        w_out[t, row0] = w_out[t, row0] + c_south * (row0_out[t] - from_south[t])
        place = 2 * (t * nz + row_z)
        spread_ghost = jnp.broadcast_to(flow_ghost, (nz, lanes))
        east_end = jnp.sum(jnp.where(lane_z == place, spread_ghost, 0.0), axis=1, keepdims=True)
        west_end = jnp.sum(jnp.where(lane_z == place + 1, spread_ghost, 0.0), axis=1, keepdims=True)
        ends = jnp.where(lane_z == lanes - 1, east_end, jnp.where(lane_z == 0, west_end, 0.0))
        north_ghost.append(from_north[3 + t] - out_north + ends)

    def complete(k, carry):
        edge_w, *dots = carry
        for t in range(2):
            v = bp[t, at(k)]
            j = t * nz + k
            w = w_out[t, at(k)] + unpack(flow, j)
            w_out[t, at(k)] = w
            dots[2 * t], dots[2 * t + 1] = dots[2 * t] + v * w, dots[2 * t + 1] + w * w
            edge_w = pack(w, j, edge_w)
        return edge_w, *dots

    edge_w, *dots = over_levels(complete, (zero,) * 5)
    for t in range(2):
        sums[t] += dots[2 * t:2 * t + 2]
        wrow_out[t] = w_out[t, row15]
    wcol_out[...] = edge_w
    gap = edge_w - ghost
    east_sum = jnp.where(even, (cross * gap) * gap, 0.0)

    def energy(k, carry):
        carry = list(carry)
        for t in range(2):
            w = w_out[t, at(k)]
            gap_east, gap_north = w - turn(w, -1), w - turn(w, -1, 0)
            gap_down = w - w_out[t, at(jnp.minimum(k + 1, nz - 1))]
            carry[t] = carry[t] + (((ce[at(k)] * gap_east) * gap_east + (cn[at(k)] * gap_north) * gap_north)
                                   + (cd[at(k + 1)] * gap_down) * gap_down)
        return tuple(carry)

    cubes = over_levels(energy, tuple(jnp.where(lane2 // (2 * nz) == t, east_sum, 0.0) for t in range(2)))
    for t in range(2):
        s3 = cubes[t]
        gap = wrow_out[t] - north_ghost[t]
        out_north = c_north * gap
        zrow_north[t] = out_north
        row_sum = out_north * gap
        for k in range(nz // rows):
            s3 = s3 + row_sum[k * rows:(k + 1) * rows]
        sums[t].append(s3)

    mine = jnp.zeros((rows // 2, lanes), jnp.float32)
    for t in range(2):
        for j in range(4):
            one = jnp.sum(sums[t][j][:rows // 2] + sums[t][j][rows // 2:], axis=1, keepdims=True)
            mine = jnp.where(lane2[:rows // 2] == t * 4 + j, one, mine)
    mine = jnp.sum(mine, axis=0, keepdims=True)
    part[0] = mine

    @pl.when(jnp.logical_not(is_hub))
    def _():
        slot = lax.rem(lat - HUB + nlat, nlat)
        give = pltpu.make_async_remote_copy(
            part.at[0], hub_in.at[slot], hub_send.at[0], hub_recv.at[0],
            device_id={"lat": HUB}, device_id_type=MESH)
        give.start()
        give.wait_send()
    later = [
        send(wcol_out, wcol_west, 8, east),
        send(wrow_out, wrow_south, 9, north),
    ]
    for copy in later:
        copy.wait_recv()
    flow = cross * (edge_w - jnp.where(even, ghost, turn(wcol_west[...], 1)))

    @over_levels
    def _(k, carry):
        for t in range(2):
            z_out[t, at(k)] = inside(w_out, t, k)[1] + unpack(flow, t * nz + k)
        return carry

    for t in range(2):
        z_out[t, row15] = z_out[t, row15] + zrow_north[t]
        z_out[t, row0] = z_out[t, row0] + c_south * (w_out[t, row0] - wrow_south[t])

    @pl.when(jnp.logical_not(is_hub))
    def _():
        pltpu.make_async_copy(total.at[0], total.at[0], hub_recv.at[2]).wait()

    @pl.when(is_hub)
    def _():
        members = hub_in.at[pl.ds(1, nlat - 1)]
        peers = peer_in.at[pl.ds(1, nlon - 1)]
        hub_in[0] = part[0]
        pltpu.make_async_copy(members, members, hub_recv.at[0]).wait()
        peer_in[0] = jnp.sum(hub_in[...], axis=0)

        for d in range(1, nlon):
            pltpu.make_async_remote_copy(
                peer_in.at[0], peer_in.at[d], hub_send.at[1], hub_recv.at[1],
                device_id={"lon": lax.rem(lon + d, nlon)}, device_id_type=MESH).start()
        pltpu.make_async_copy(peers, peers, hub_recv.at[1]).wait()
        total[0] = jnp.sum(peer_in[...], axis=0)

        for d in range(1, nlat):
            pltpu.make_async_remote_copy(
                total.at[0], total.at[0], hub_send.at[2], hub_recv.at[2],
                device_id={"lat": (HUB + d) % nlat}, device_id_type=MESH).start()

    got = total[0]
    for t in range(2):
        m0, l1, l2, l3 = [jnp.sum(jnp.where(lane1 == t * 4 + j, got, 0.0), axis=1, keepdims=True) for j in range(4)]
        c0 = l1 / m0
        a0 = m0 / (m0 + l1)
        spread = l2 - l1 * c0
        curve = l3 - c0 * (2.0 * l2 - c0 * l1)
        beta = a0 * a0 * spread / m0
        a1 = spread / (spread + curve - a0 * spread * (spread / m0))
        g = a0 * c0 + beta
        values = (a0 + a1 * g, -a1 * a0, a0 * c0 - a1 * g, a1 * a0 - a0 - a1 * g, a1 * a0)
        for coef, value in zip((coef0, coef1, coef2, coef3, coef4), values, strict=True):
            coef[t:t + 1] = jnp.broadcast_to(value, (1, lanes))

    for copy in halo + later:
        copy.wait_send()

    @pl.when(is_hub)
    def _():
        peers, members = peer_in.at[pl.ds(1, nlon - 1)], hub_in.at[pl.ds(1, nlat - 1)]
        pltpu.make_async_copy(peers, peers, hub_send.at[1]).wait()
        pltpu.make_async_copy(members, members, hub_send.at[2]).wait()


def finish(b, w, z, coef0, coef1, coef2, coef3, coef4, x_out, r_out, x, r, sem):
    part = b.shape[1] // PARTS
    copies = []
    for t in range(2):
        one = slice(t, t + 1)
        for n in range(PARTS):
            at = (t, pl.ds(n * part, part))
            x[at] = coef0[one] * b[at] + coef1[one] * w[at]
            r[at] = (coef2[one] * b[at] + coef3[one] * w[at]) + coef4[one] * z[at]
            for source, target in ((x, x_out), (r, r_out)):
                copies.append(pltpu.make_async_copy(source.at[at], target.at[at], sem.at[len(copies)]))
                copies[-1].start()
    for copy in copies:
        copy.wait()


def solution(mesh):
    nlon, nlat = mesh.shape["lon"], mesh.shape["lat"]

    def body(rhs, sea_mask, levels, ed, nd, vd):
        tracers, nz, rows, lanes = rhs.shape
        field, block = (tracers, nz * rows, lanes), (nz * rows, lanes)
        taller = ((nz + 1) * rows, lanes)
        flat = [rhs.reshape(field), sea_mask.reshape(block), levels] + [one.reshape(block) for one in (ed, nd, vd)]
        f32 = jnp.float32
        whole = pl.BlockSpec(memory_space=pltpu.VMEM)
        fields = pl.pallas_call(
            lambda *refs: kernel(nlon, nlat, *refs),
            out_shape=(jax.ShapeDtypeStruct(field, f32),) * 3 + (jax.ShapeDtypeStruct((tracers, lanes), f32),) * 5,
            in_specs=[pl.BlockSpec(memory_space=pltpu.HBM)] * 6,
            out_specs=(whole,) * 8,
            scratch_shapes=[
                pltpu.VMEM(block, jnp.int32), pltpu.VMEM((rows, lanes), jnp.int32),
                pltpu.VMEM(block, jnp.bfloat16), pltpu.VMEM(block, jnp.bfloat16), pltpu.VMEM(block, jnp.bfloat16),
                pltpu.VMEM(taller, f32), pltpu.VMEM(block, f32), pltpu.VMEM(block, f32),
                pltpu.VMEM(block, f32), pltpu.VMEM(block, f32), pltpu.VMEM(block, f32), pltpu.VMEM(block, f32),
                pltpu.VMEM(taller, f32),
                pltpu.VMEM((4, rows, lanes), f32), pltpu.VMEM((4, rows, lanes), f32), pltpu.VMEM((2, rows, lanes), f32),
                pltpu.VMEM((5, nz, lanes), f32), pltpu.VMEM((3, nz, lanes), f32),
                pltpu.VMEM((5, nz, lanes), f32), pltpu.VMEM((3, nz, lanes), f32),
                pltpu.VMEM((2, 2, 1, lanes), f32), pltpu.VMEM((4, 2, 1, lanes), f32),
                pltpu.VMEM((rows, lanes), f32), pltpu.VMEM((rows, lanes), f32),
                pltpu.VMEM((2, nz, lanes), f32), pltpu.VMEM((2, nz, lanes), f32), pltpu.VMEM((2, nz, lanes), f32),
                pltpu.VMEM((1, 1, lanes), f32), pltpu.VMEM((nlat, 1, lanes), f32),
                pltpu.VMEM((nlon, 1, lanes), f32), pltpu.VMEM((1, 1, lanes), f32),
                pltpu.SemaphoreType.DMA((6,)), pltpu.SemaphoreType.DMA((10,)), pltpu.SemaphoreType.DMA((10,)),
                pltpu.SemaphoreType.DMA((3,)), pltpu.SemaphoreType.DMA((3,)),
            ],
            compiler_params=pltpu.CompilerParams(collective_id=0, has_side_effects=True, vmem_limit_bytes=32 * 1024 * 1024),
        )(*[pltpu.with_memory_space_constraint(one, pltpu.HBM) for one in flat])
        in_place = pl.BlockSpec(memory_space=pltpu.HBM)
        solved = pl.pallas_call(
            finish,
            out_shape=(jax.ShapeDtypeStruct(field, f32),) * 2,
            in_specs=[whole] * 8,
            out_specs=(in_place,) * 2,
            scratch_shapes=[pltpu.VMEM(field, f32), pltpu.VMEM(field, f32), pltpu.SemaphoreType.DMA((4 * PARTS,))],
            compiler_params=pltpu.CompilerParams(vmem_limit_bytes=16 * 1024 * 1024),
        )(*fields)
        return tuple(one.reshape(rhs.shape) for one in solved)

    return jax.shard_map(
        body,
        mesh=mesh,
        in_specs=(
            P(None, None, "lat", "lon"),
            P(None, "lat", "lon"),
            P("lat", "lon"),
            P(None, "lat", "lon"),
            P(None, "lat", "lon"),
            P(None, "lat", "lon"),
        ),
        out_specs=(P(None, None, "lat", "lon"), P(None, None, "lat", "lon")),
        check_vma=False,
    )
```

```python
import jax
import jax.numpy as jnp
from jax import lax
from jax.experimental import pallas as pl
from jax.experimental.pallas import tpu as pltpu
from jax.sharding import PartitionSpec as P

MESH = pl.DeviceIdType.MESH
UNROLL = 16
PARTS = 2
HUB = 1


def kernel(nlon, nlat, rhs, mask_in, levels_in, ed_in, nd_in, vd_in,
           bp, w_out, z_out, coef0, coef1, coef2, coef3, coef4,
           maskv, levelsv, edv, ndv, vdv,
           ocp, edp, ndp, ce, cw, cn, cs, cd,
           col_out, from_east, from_west,
           row0_out, row15_out, from_north, from_south,
           corner_out, corner_in, wcol_out, wcol_west, wrow_out, wrow_south, zrow_north,
           part, hub_in, peer_in, total,
           in_sem, send_sem, recv_sem, hub_send, hub_recv):
    rows, lanes = levels_in.shape
    nz = mask_in.shape[0] // rows
    lon, lat = lax.axis_index("lon"), lax.axis_index("lat")
    lon_east, lon_west = lax.rem(lon + 1, nlon), lax.rem(lon + nlon - 1, nlon)
    lat_north, lat_south = lax.rem(lat + 1, nlat), lax.rem(lat + nlat - 1, nlat)
    east, west = {"lon": lon_east}, {"lon": lon_west}
    north, south = {"lat": lat_north}, {"lat": lat_south}
    north_east = {"lon": lon_east, "lat": lat_north}
    north_west = {"lon": lon_west, "lat": lat_north}
    south_east = {"lon": lon_east, "lat": lat_south}
    south_west = {"lon": lon_west, "lat": lat_south}
    is_hub = lat == HUB

    barrier = pltpu.get_barrier_semaphore()
    for target in (east, west, north, south, north_east, north_west, south_east):
        pl.semaphore_signal(barrier, 1, device_id=target, device_id_type=MESH)

    loads = [
        pltpu.make_async_copy(mask_in, maskv, in_sem.at[0]),
        pltpu.make_async_copy(levels_in, levelsv, in_sem.at[1]),
        pltpu.make_async_copy(ed_in, edv, in_sem.at[2]),
        pltpu.make_async_copy(nd_in, ndv, in_sem.at[3]),
        pltpu.make_async_copy(vd_in, vdv, in_sem.at[4]),
        pltpu.make_async_copy(rhs, bp, in_sem.at[5]),
    ]
    for load in loads:
        load.start()

    @pl.when(is_hub)
    def _():
        def tell_member(d, carry):
            pl.semaphore_signal(barrier, 1, device_id={"lat": lax.rem(lat + d, nlat)}, device_id_type=MESH)
            return carry

        lax.fori_loop(1, nlat, tell_member, 0)

        def tell_peer(d, carry):
            pl.semaphore_signal(barrier, 1, device_id={"lon": lax.rem(lon + d, nlon)}, device_id_type=MESH)
            return carry

        lax.fori_loop(1, nlon, tell_peer, 0)

    lane2 = lax.broadcasted_iota(jnp.int32, (rows, lanes), 1)
    row2 = lax.broadcasted_iota(jnp.int32, (rows, lanes), 0)
    lane1 = lax.broadcasted_iota(jnp.int32, (1, lanes), 1)
    lane_z = lax.broadcasted_iota(jnp.int32, (nz, lanes), 1)
    row_z = lax.broadcasted_iota(jnp.int32, (nz, lanes), 0)
    first_row, last_row = row2 == 0, row2 == rows - 1
    first_lane, last_lane = lane2 == 0, lane2 == lanes - 1
    edge_lane = first_lane | last_lane
    pair = lane2 // 2
    even, even1 = lane2 % 2 == 0, lane1 % 2 == 0
    zero = jnp.zeros((rows, lanes), jnp.float32)

    def at(k):
        return pl.ds(pl.multiple_of(k * rows, rows), rows)

    def over_levels(step, carry=0, unroll=UNROLL):
        def several(n, carry):
            for i in range(unroll):
                carry = step(n * unroll + i, carry)
            return carry

        return lax.fori_loop(0, nz // unroll, several, carry)

    row0, row15 = pl.ds(0, nz, stride=rows), pl.ds(rows - 1, nz, stride=rows)

    def turn(piece, shift, axis=1):
        if isinstance(shift, int):
            shift = shift % piece.shape[axis]
        return pltpu.roll(piece, shift, axis)

    def pack(piece, j, into):
        return jnp.where(pair == j, turn(piece, 2 * j + 1), into)

    def unpack(packed, j):
        return jnp.where(edge_lane, turn(packed, lanes - 1 - 2 * j), 0.0)

    def facing(east_packed, west_packed):
        return jnp.where(even if east_packed.shape[0] == rows else even1, turn(east_packed, -1), turn(west_packed, 1))

    def both(packed):
        return packed + turn(packed, 2 * nz)

    def inside(field, t, k):
        v = field[t, at(k)]
        flows = (ce[at(k)] * (v - turn(v, -1)) + cw[at(k)] * (v - turn(v, 1))) + (
            cn[at(k)] * (v - turn(v, -1, 0)) + cs[at(k)] * (v - turn(v, 1, 0)))
        below, above = field[t, at(jnp.minimum(k + 1, nz - 1))], field[t, at(jnp.maximum(k - 1, 0))]
        return v, flows + (cd[at(k + 1)] * (v - below) + cd[at(k)] * (v - above))

    loads[0].wait()
    loads[1].wait()
    @over_levels
    def _(k, carry):
        ocp[at(k)] = jnp.where((maskv[at(k)] == 1) & (levelsv[...] > k), 1.0, 0.0)
        return carry

    ocp[at(nz)] = zero
    cd[at(0)] = zero
    for load in loads[2:5]:
        load.wait()

    @over_levels
    def _(k, carry):
        oc = ocp[at(k)]
        edp[at(k)] = edv[at(k)].astype(jnp.float32) * oc
        ndp[at(k)] = ndv[at(k)].astype(jnp.float32) * oc
        cd[at(k + 1)] = vdv[at(k)].astype(jnp.float32) * oc * ocp[at(k + 1)]
        return carry

    def faces(k, carry):
        edge_coef, edge_nd = carry
        oc, ed, nd = ocp[at(k)], edp[at(k)], ndp[at(k)]
        ce[at(k)] = jnp.where(last_lane, 0.0, ed * turn(oc, -1))
        cw[at(k)] = jnp.where(first_lane, 0.0, turn(ed, 1) * oc)
        cn[at(k)] = jnp.where(last_row, 0.0, nd * turn(oc, -1, 0))
        cs[at(k)] = jnp.where(first_row, 0.0, turn(nd, 1, 0) * oc)
        return pack(jnp.where(last_lane, ed, oc), k, edge_coef), pack(nd, k, edge_nd)

    edge_coef, edge_nd = over_levels(faces, (zero, zero))
    edge_coef, edge_nd = both(edge_coef), both(edge_nd)
    row0_out[2] = ocp[row0]
    row15_out[2] = ndp[row15]
    loads[5].wait()

    def inner(k, carry):
        edge_b, edge_p, *squares = carry
        for t in range(2):
            v, flows = inside(bp, t, k)
            w_out[t, at(k)] = flows
            squares[t] = squares[t] + v * v
            j = t * nz + k
            edge_b, edge_p = pack(v, j, edge_b), pack(flows, j, edge_p)
        return edge_b, edge_p, *squares

    edge_b, edge_p, *squares = over_levels(inner, (zero,) * 4, nz)
    sums = [[one] for one in squares]
    for t in range(2):
        row0_out[t] = bp[t, row0]
        row15_out[t] = bp[t, row15]
        row0_out[3 + t] = w_out[t, row0]
    col_out[0], col_out[1], col_out[2], col_out[3] = edge_b, edge_coef, edge_p, edge_nd
    corner_out[0, 0], corner_out[0, 1] = edge_b[0:1], edge_coef[0:1]
    corner_out[1, 0], corner_out[1, 1] = edge_b[rows - 1:rows], edge_nd[rows - 1:rows]

    pl.semaphore_wait(barrier, jnp.where(is_hub, nlon + 6, 8))

    def send(source, target, number, device):
        copy = pltpu.make_async_remote_copy(
            source, target, send_sem.at[number], recv_sem.at[number], device_id=device, device_id_type=MESH)
        copy.start()
        return copy

    halo = [
        send(corner_out.at[0], corner_in.at[1], 2, south_west),
        send(corner_out.at[0], corner_in.at[2], 3, south_east),
        send(corner_out.at[1], corner_in.at[3], 4, north_west),
        send(corner_out.at[0], corner_in.at[0], 5, south),
        send(row0_out, from_north, 6, south),
        send(row15_out, from_south, 7, north),
        send(col_out, from_east, 0, west),
        send(col_out.at[pl.ds(0, 2)], from_west, 1, east),
    ]
    for copy in halo:
        copy.wait_recv()

    top = jnp.where(lat == nlat - 1, 0.0, 1.0)
    bottom = jnp.where(lat == 0, 0.0, 1.0)
    cross = edge_coef * facing(from_east[1], from_west[1])
    faced_b = facing(from_east[0], from_west[0])
    flow = cross * (edge_b - faced_b)
    ghost = turn(from_east[2], -1) - flow
    ne_b, ne_oc = turn(corner_in[1, 0], -1), turn(corner_in[1, 1], -1)
    se_b, se_nd = turn(corner_in[3, 0], -1), turn(corner_in[3, 1], -1)
    east_oc, east_nd = turn(from_east[1], -1), turn(from_east[3], -1)
    ghost = ghost + jnp.where(last_row, (east_nd * (ne_oc * top)) * (faced_b - ne_b), 0.0)
    ghost = ghost + jnp.where(first_row, (east_oc * (se_nd * bottom)) * (faced_b - se_b), 0.0)
    flow_ghost = (corner_in[0, 1] * facing(corner_in[1, 1], corner_in[2, 1])) * (
        corner_in[0, 0] - facing(corner_in[1, 0], corner_in[2, 0]))
    c_north = row15_out[2] * (from_north[2] * top)
    c_south = (from_south[2] * bottom) * row0_out[2]
    north_ghost = []
    for t in range(2):
        out_north = c_north * (row15_out[t] - from_north[t])
        w_out[t, row15] = w_out[t, row15] + out_north
        w_out[t, row0] = w_out[t, row0] + c_south * (row0_out[t] - from_south[t])
        place = 2 * (t * nz + row_z)
        spread_ghost = jnp.broadcast_to(flow_ghost, (nz, lanes))
        east_end = jnp.sum(jnp.where(lane_z == place, spread_ghost, 0.0), axis=1, keepdims=True)
        west_end = jnp.sum(jnp.where(lane_z == place + 1, spread_ghost, 0.0), axis=1, keepdims=True)
        ends = jnp.where(lane_z == lanes - 1, east_end, jnp.where(lane_z == 0, west_end, 0.0))
        north_ghost.append(from_north[3 + t] - out_north + ends)

    def complete(k, carry):
        edge_w, *dots = carry
        for t in range(2):
            v = bp[t, at(k)]
            j = t * nz + k
            w = w_out[t, at(k)] + unpack(flow, j)
            w_out[t, at(k)] = w
            dots[2 * t], dots[2 * t + 1] = dots[2 * t] + v * w, dots[2 * t + 1] + w * w
            edge_w = pack(w, j, edge_w)
        return edge_w, *dots

    edge_w, *dots = over_levels(complete, (zero,) * 5)
    for t in range(2):
        sums[t] += dots[2 * t:2 * t + 2]
        wrow_out[t] = w_out[t, row15]
    wcol_out[...] = edge_w
    gap = edge_w - ghost
    east_sum = jnp.where(even, (cross * gap) * gap, 0.0)

    def energy(k, carry):
        carry = list(carry)
        for t in range(2):
            w = w_out[t, at(k)]
            gap_east, gap_north = w - turn(w, -1), w - turn(w, -1, 0)
            gap_down = w - w_out[t, at(jnp.minimum(k + 1, nz - 1))]
            carry[t] = carry[t] + (((ce[at(k)] * gap_east) * gap_east + (cn[at(k)] * gap_north) * gap_north)
                                   + (cd[at(k + 1)] * gap_down) * gap_down)
        return tuple(carry)

    cubes = over_levels(energy, tuple(jnp.where(lane2 // (2 * nz) == t, east_sum, 0.0) for t in range(2)))
    for t in range(2):
        s3 = cubes[t]
        gap = wrow_out[t] - north_ghost[t]
        out_north = c_north * gap
        zrow_north[t] = out_north
        row_sum = out_north * gap
        for k in range(nz // rows):
            s3 = s3 + row_sum[k * rows:(k + 1) * rows]
        sums[t].append(s3)

    mine = jnp.zeros((rows // 2, lanes), jnp.float32)
    for t in range(2):
        for j in range(4):
            one = jnp.sum(sums[t][j][:rows // 2] + sums[t][j][rows // 2:], axis=1, keepdims=True)
            mine = jnp.where(lane2[:rows // 2] == t * 4 + j, one, mine)
    mine = jnp.sum(mine, axis=0, keepdims=True)
    part[0] = mine

    @pl.when(jnp.logical_not(is_hub))
    def _():
        slot = lax.rem(lat - HUB + nlat, nlat)
        give = pltpu.make_async_remote_copy(
            part.at[0], hub_in.at[slot], hub_send.at[0], hub_recv.at[0],
            device_id={"lat": HUB}, device_id_type=MESH)
        give.start()
        give.wait_send()
    later = [
        send(wcol_out, wcol_west, 8, east),
        send(wrow_out, wrow_south, 9, north),
    ]
    for copy in later:
        copy.wait_recv()
    flow = cross * (edge_w - jnp.where(even, ghost, turn(wcol_west[...], 1)))

    @over_levels
    def _(k, carry):
        for t in range(2):
            z_out[t, at(k)] = inside(w_out, t, k)[1] + unpack(flow, t * nz + k)
        return carry

    for t in range(2):
        z_out[t, row15] = z_out[t, row15] + zrow_north[t]
        z_out[t, row0] = z_out[t, row0] + c_south * (w_out[t, row0] - wrow_south[t])

    @pl.when(jnp.logical_not(is_hub))
    def _():
        pltpu.make_async_copy(total.at[0], total.at[0], hub_recv.at[2]).wait()

    @pl.when(is_hub)
    def _():
        members = hub_in.at[pl.ds(1, nlat - 1)]
        peers = peer_in.at[pl.ds(1, nlon - 1)]
        hub_in[0] = part[0]
        pltpu.make_async_copy(members, members, hub_recv.at[0]).wait()
        peer_in[0] = jnp.sum(hub_in[...], axis=0)

        for d in range(1, nlon):
            pltpu.make_async_remote_copy(
                peer_in.at[0], peer_in.at[d], hub_send.at[1], hub_recv.at[1],
                device_id={"lon": lax.rem(lon + d, nlon)}, device_id_type=MESH).start()
        pltpu.make_async_copy(peers, peers, hub_recv.at[1]).wait()
        total[0] = jnp.sum(peer_in[...], axis=0)

        for d in range(1, nlat):
            pltpu.make_async_remote_copy(
                total.at[0], total.at[0], hub_send.at[2], hub_recv.at[2],
                device_id={"lat": (HUB + d) % nlat}, device_id_type=MESH).start()

    got = total[0]
    for t in range(2):
        m0, l1, l2, l3 = [jnp.sum(jnp.where(lane1 == t * 4 + j, got, 0.0), axis=1, keepdims=True) for j in range(4)]
        c0 = l1 / m0
        a0 = m0 / (m0 + l1)
        spread = l2 - l1 * c0
        curve = l3 - c0 * (2.0 * l2 - c0 * l1)
        beta = a0 * a0 * spread / m0
        a1 = spread / (spread + curve - a0 * spread * (spread / m0))
        g = a0 * c0 + beta
        values = (a0 + a1 * g, -a1 * a0, a0 * c0 - a1 * g, a1 * a0 - a0 - a1 * g, a1 * a0)
        for coef, value in zip((coef0, coef1, coef2, coef3, coef4), values, strict=True):
            coef[t:t + 1] = jnp.broadcast_to(value, (1, lanes))

    for copy in halo + later:
        copy.wait_send()

    @pl.when(is_hub)
    def _():
        peers, members = peer_in.at[pl.ds(1, nlon - 1)], hub_in.at[pl.ds(1, nlat - 1)]
        pltpu.make_async_copy(peers, peers, hub_send.at[1]).wait()
        pltpu.make_async_copy(members, members, hub_send.at[2]).wait()


def finish(b, w, z, coef0, coef1, coef2, coef3, coef4, x_out, r_out, x, r, sem):
    part = b.shape[1] // PARTS
    copies = []
    for t in range(2):
        one = slice(t, t + 1)
        for n in range(PARTS):
            at = (t, pl.ds(n * part, part))
            x[at] = coef0[one] * b[at] + coef1[one] * w[at]
            r[at] = (coef2[one] * b[at] + coef3[one] * w[at]) + coef4[one] * z[at]
            for source, target in ((x, x_out), (r, r_out)):
                copies.append(pltpu.make_async_copy(source.at[at], target.at[at], sem.at[len(copies)]))
                copies[-1].start()
    for copy in copies:
        copy.wait()


def solution(mesh):
    nlon, nlat = mesh.shape["lon"], mesh.shape["lat"]

    def body(rhs, sea_mask, levels, ed, nd, vd):
        tracers, nz, rows, lanes = rhs.shape
        field, block = (tracers, nz * rows, lanes), (nz * rows, lanes)
        taller = ((nz + 1) * rows, lanes)
        flat = [rhs.reshape(field), sea_mask.reshape(block), levels] + [one.reshape(block) for one in (ed, nd, vd)]
        f32 = jnp.float32
        whole = pl.BlockSpec(memory_space=pltpu.VMEM)
        fields = pl.pallas_call(
            lambda *refs: kernel(nlon, nlat, *refs),
            out_shape=(jax.ShapeDtypeStruct(field, f32),) * 3 + (jax.ShapeDtypeStruct((tracers, lanes), f32),) * 5,
            in_specs=[pl.BlockSpec(memory_space=pltpu.HBM)] * 6,
            out_specs=(whole,) * 8,
            scratch_shapes=[
                pltpu.VMEM(block, jnp.int32), pltpu.VMEM((rows, lanes), jnp.int32),
                pltpu.VMEM(block, jnp.bfloat16), pltpu.VMEM(block, jnp.bfloat16), pltpu.VMEM(block, jnp.bfloat16),
                pltpu.VMEM(taller, f32), pltpu.VMEM(block, f32), pltpu.VMEM(block, f32),
                pltpu.VMEM(block, f32), pltpu.VMEM(block, f32), pltpu.VMEM(block, f32), pltpu.VMEM(block, f32),
                pltpu.VMEM(taller, f32),
                pltpu.VMEM((4, rows, lanes), f32), pltpu.VMEM((4, rows, lanes), f32), pltpu.VMEM((2, rows, lanes), f32),
                pltpu.VMEM((5, nz, lanes), f32), pltpu.VMEM((3, nz, lanes), f32),
                pltpu.VMEM((5, nz, lanes), f32), pltpu.VMEM((3, nz, lanes), f32),
                pltpu.VMEM((2, 2, 1, lanes), f32), pltpu.VMEM((4, 2, 1, lanes), f32),
                pltpu.VMEM((rows, lanes), f32), pltpu.VMEM((rows, lanes), f32),
                pltpu.VMEM((2, nz, lanes), f32), pltpu.VMEM((2, nz, lanes), f32), pltpu.VMEM((2, nz, lanes), f32),
                pltpu.VMEM((1, 1, lanes), f32), pltpu.VMEM((nlat, 1, lanes), f32),
                pltpu.VMEM((nlon, 1, lanes), f32), pltpu.VMEM((1, 1, lanes), f32),
                pltpu.SemaphoreType.DMA((6,)), pltpu.SemaphoreType.DMA((10,)), pltpu.SemaphoreType.DMA((10,)),
                pltpu.SemaphoreType.DMA((3,)), pltpu.SemaphoreType.DMA((3,)),
            ],
            compiler_params=pltpu.CompilerParams(collective_id=0, has_side_effects=True, vmem_limit_bytes=32 * 1024 * 1024),
        )(*[pltpu.with_memory_space_constraint(one, pltpu.HBM) for one in flat])
        in_place = pl.BlockSpec(memory_space=pltpu.HBM)
        solved = pl.pallas_call(
            finish,
            out_shape=(jax.ShapeDtypeStruct(field, f32),) * 2,
            in_specs=[whole] * 8,
            out_specs=(in_place,) * 2,
            scratch_shapes=[pltpu.VMEM(field, f32), pltpu.VMEM(field, f32), pltpu.SemaphoreType.DMA((4 * PARTS,))],
            compiler_params=pltpu.CompilerParams(vmem_limit_bytes=16 * 1024 * 1024),
        )(*fields)
        return tuple(one.reshape(rhs.shape) for one in solved)

    return jax.shard_map(
        body,
        mesh=mesh,
        in_specs=(
            P(None, None, "lat", "lon"),
            P(None, "lat", "lon"),
            P("lat", "lon"),
            P(None, "lat", "lon"),
            P(None, "lat", "lon"),
            P(None, "lat", "lon"),
        ),
        out_specs=(P(None, None, "lat", "lon"), P(None, None, "lat", "lon")),
        check_vma=False,
    )
```
